256 devices in a mesh: tm: 16 (over x_lo, z), sensor: 16 (over x_hi, y, core).
Axes of the slice: x: 4 (x_hi: 2, x_lo: 2; x = x_hi * 2 + x_lo), y: 4, z: 8, core: 2. Of those that a mesh axis runs over, the one named last changes fastest.
Arguments:
- state_tiles: bfloat16 [32768, 8192], P('sensor', 'tm'), may hold values from -6 to 6
- sketch: bfloat16 [1024, 128], replicated, may hold values from -0.1875 to 0.1875
- probe_cell: int32 [16, 16, 32], P('sensor'), may hold values from 0 to 2047
- probe_row: int32 [16, 16, 32], P('sensor'), may hold values from -1 to 255, as said below
Outputs:
- hankel_sketch: float32 [512, 4096, 128], P('tm', 'sensor')
- column_image: float32 [1024, 128], P(('tm', 'sensor'))
The draws below stay inside these ranges and needn't reach their ends.
Inputs may be any that keep to these rules, and one draw needn't show every extreme that they name: `probe_row`: every sensor row of every owner is filled by exactly one slot over all tiles; for each owner, the tiles that feed it fill all 32 of their slots to it and the other tiles none, and exactly half of the tiles feed each owner.
All inputs are finite; a program needn't handle non-finite values.
Results may differ from the reference program's by a relative error of at most 0.0003.
Values may be sent and summed in bfloat16 or wider, within the bound.
A program may use at most 64 MiB of HBM per device.

```python
import math
import jax
import jax.numpy as jnp
from jax import lax

INPUTS = 16
SENS_DEV = 256
SK = 128
CELLS_DEV = 2048
SENSORS = 4096
STEPS = 512
KC = 64
CELLS = 32768
TILES = 16
CAPD = 32
N_SENSOR = 16


def draw_probe_row(key, part):
    key_bias, key_jitter, key_shuffle = jax.random.split(jax.random.fold_in(key, 7), 3)
    heaviness = jax.random.randint(key_bias, (TILES,), 0, 4)
    jitter = jax.random.randint(key_jitter, (TILES, TILES), 0, 6)
    scores = (heaviness[None, :] * 6 + jitter) * TILES + jnp.arange(TILES, dtype=jnp.int32)[None, :]
    ranking = jnp.argsort(-scores, axis=1, stable=True)
    tile_rank = jnp.argsort(ranking, axis=1, stable=True).astype(jnp.int32)
    shuffled = jax.vmap(lambda k: jax.random.permutation(k, SENS_DEV))(jax.random.split(key_shuffle, TILES)).astype(jnp.int32)
    slot_ids = jnp.arange(CAPD, dtype=jnp.int32)
    position = jnp.minimum(tile_rank[:, :, None], TILES // 2 - 1) * CAPD + slot_ids[None, None, :]
    picked = jnp.take_along_axis(shuffled, position.reshape(TILES, TILES * CAPD), axis=1).reshape(TILES, TILES, CAPD)
    return jnp.where(tile_rank[:, :, None] < TILES // 2, picked, -1).astype(jnp.int32)


def set_ends(entries, own_key, smallest, largest):
    extent = entries.shape
    place = [jax.random.randint(jax.random.fold_in(own_key, axis), (), 0, extent[axis]) for axis in range(len(extent))]
    entries = entries.at[tuple(place)].set(smallest)
    longest = extent.index(max(extent))
    place[longest] = (place[longest] + 1) % extent[longest]
    return entries.at[tuple(place)].set(largest)


def block_scale(rng, dims, cuts, least, largest):
    level = 1.0
    for dim, parts in cuts:
        steps = jax.random.uniform(jax.random.fold_in(jax.random.fold_in(rng, 6), dim), (parts,), jnp.float32, least / len(cuts), largest / len(cuts))
        level = level * jnp.repeat(jnp.exp(steps), dims[dim] // parts).reshape((-1,) + (1,) * (len(dims) - 1 - dim))
    return level


def gaussian(rng, shape, deviation, bound, pieces=(), kind=jnp.bfloat16):
    level = block_scale(rng, shape, pieces, -0.22, 0.18) if pieces else 1.0
    result = jax.random.normal(rng, shape, jnp.float32) * deviation * level
    return jnp.minimum(jnp.maximum(result, -bound), bound).astype(kind)


def setup_inputs(seed: int = 0) -> dict:
    splits = jax.random.split(jax.random.key(seed), 5)
    state_tiles = gaussian(splits[0], (CELLS, STEPS * INPUTS), 1.0, 6.0, ((0, 16), (1, 16)))
    sketch = gaussian(splits[1], (KC * INPUTS, SK), (KC * INPUTS) ** -0.5, 0.1875)
    probe_cell = set_ends(jax.random.randint(splits[2], (N_SENSOR, N_SENSOR, CAPD), 0, CELLS_DEV), jax.random.fold_in(splits[2], 1), 0, CELLS_DEV - 1).astype(jnp.int32)
    probe_row = draw_probe_row(jax.random.fold_in(splits[4], 71), 0)
    return {"state_tiles": state_tiles, "sketch": sketch, "probe_cell": probe_cell, "probe_row": probe_row}


def reference(state_tiles, sketch, probe_cell, probe_row):
    tile_ids = jnp.arange(N_SENSOR, dtype=jnp.int32)
    source = (tile_ids[:, None, None] * CELLS_DEV + probe_cell).reshape(-1)
    rows_tile = jnp.transpose(probe_row, (1, 0, 2))
    target = jnp.where(rows_tile >= 0, tile_ids[None, :, None] * SENS_DEV + rows_tile, SENSORS).reshape(-1)
    outputs = jnp.zeros((SENSORS, STEPS * INPUTS), jnp.bfloat16).at[target].set(state_tiles[source], mode='drop')
    padded = jnp.concatenate([outputs, jnp.zeros((SENSORS, KC * INPUTS), jnp.bfloat16)], axis=1)
    group_size = math.gcd(STEPS, 8)
    sketch_wide = sketch.astype(jnp.float32)

    def one_block(total, block):
        starts = block * group_size + jnp.arange(group_size, dtype=jnp.int32)
        windows = jax.vmap(lambda first: lax.dynamic_slice_in_dim(padded, first * INPUTS, KC * INPUTS, 1))(starts)
        windows = windows.astype(jnp.float32)
        image = jnp.einsum('isk,kc->isc', windows, sketch_wide)
        image_bf = lax.optimization_barrier(image.astype(jnp.bfloat16)).astype(jnp.float32)
        total = total + jnp.einsum('isk,isc->kc', windows, image_bf)
        return (total, image)
    total, images = lax.scan(one_block, jnp.zeros((KC * INPUTS, SK), jnp.float32), jnp.arange(STEPS // group_size, dtype=jnp.int32))
    hankel_sketch = images.reshape(STEPS, SENSORS, SK)
    column_image = total * (1.0 / math.sqrt(SENSORS * STEPS))
    return (hankel_sketch, column_image)
```

```python
import functools
import math

import jax
import jax.numpy as jnp
from jax import lax
from jax.experimental import pallas as pl
from jax.experimental.pallas import tpu as pltpu
from jax.sharding import PartitionSpec as P

INPUTS = 16
KC = 64
LANES = 128
MESH = pl.DeviceIdType.MESH
F32 = jnp.float32
BF16 = jnp.bfloat16


def dot(a, b):
    return jnp.dot(a, b, preferred_element_type=F32)


def kernel(
    n_tm, n_sn, n_xl, n_xh, scale,
    state, sketch, cell, row, hank, col,
    st, sk, cellv, rowv, one, put, sendb, arr, hx, ht, big, hb, rb, acc2, tot, s0b, mid, s1b, m2, s2b,
    ld_sem, a_send, a_recv, h_send, h_recv, out_sem, s0_send, s0_recv, s1_send, s1_recv, s2_send, s2_recv,
):
    t = lax.axis_index("tm")
    s = lax.axis_index("sensor")
    n_z = n_tm // n_xl
    n_xy = n_sn // 2
    zh = n_z // 2
    xl = t // n_z
    z = lax.rem(t, n_z)
    xy = s // 2
    k = lax.rem(s, 2)
    cap = cellv.shape[2]
    sd = hx.shape[1]
    span = sk.shape[0]
    cells = st.shape[0]

    loads = [
        pltpu.make_async_copy(cell, cellv, ld_sem.at[0]),
        pltpu.make_async_copy(row, rowv, ld_sem.at[1]),
        pltpu.make_async_copy(state.at[:, pl.ds(0, 256)], st.at[:, pl.ds(0, 256)], ld_sem.at[2]),
        pltpu.make_async_copy(state.at[:, pl.ds(256, 256)], st.at[:, pl.ds(256, 256)], ld_sem.at[3]),
        pltpu.make_async_copy(sketch, sk, ld_sem.at[4]),
    ]
    for c in loads:
        c.start()

    barrier = pltpu.get_barrier_semaphore()

    def greet(tt, ss):
        pl.semaphore_signal(barrier, inc=1, device_id=(tt, ss), device_id_type=MESH)

    def greet_sensor(d, _):
        greet(t, lax.rem(s + d, n_sn))
        return 0

    lax.fori_loop(1, n_sn, greet_sensor, 0)

    @pl.when(t > 0)
    def _():
        greet(t - 1, s)

    @pl.when(t < n_tm - 1)
    def _():
        greet(t + 1, s)

    def greet_plane(d, _):
        e = lax.rem(xl * n_xy + xy + d, n_xl * n_xy)
        greet((e // n_xy) * n_z + z, lax.rem(e, n_xy) * 2 + k)
        return 0

    lax.fori_loop(1, n_xl * n_xy, greet_plane, 0)

    def greet_line(d, _):
        e = lax.rem(z * 2 + k + d, n_z * 2)
        greet(xl * n_z + e // 2, xy * 2 + lax.rem(e, 2))
        return 0

    lax.fori_loop(1, n_z * 2, greet_line, 0)
    n_greet = n_sn - 1 + n_xl * n_xy - 1 + n_z * 2 - 1

    loads[0].wait()
    eye = lax.broadcasted_iota(jnp.int32, (cap, cap), 0) == lax.broadcasted_iota(jnp.int32, (cap, cap), 1)

    def column(ref, o):
        line = ref[0, o : o + 1, :].astype(F32)
        return jnp.sum(jnp.where(eye, jnp.broadcast_to(line, (cap, cap)), 0.0), axis=1, keepdims=True)

    lane_cells = lax.broadcasted_iota(jnp.int32, (cap, cells), 1).astype(F32)
    for o in range(n_sn):
        one[o * cap : (o + 1) * cap, :] = jnp.where(column(cellv, o) == lane_cells, 1.0, 0.0).astype(BF16)

    def pick(half):
        res = dot(one[...], st[:, 256 * half : 256 * half + 256]).astype(BF16)
        sendb[2 * half] = res[:, :LANES]
        sendb[2 * half + 1] = res[:, LANES:]

    def a_copy(q, d):
        dst = lax.rem(s + d, n_sn)
        return pltpu.make_async_remote_copy(
            src_ref=sendb.at[q, pl.ds(pl.multiple_of(dst * cap, cap), cap)],
            dst_ref=arr.at[q, pl.ds(pl.multiple_of(s * cap, cap), cap)],
            send_sem=a_send.at[q, d],
            recv_sem=a_recv.at[q, s],
            device_id=(t, dst),
            device_id_type=MESH,
        )

    def a_arrival(q, src):
        return pltpu.make_async_remote_copy(
            src_ref=sendb.at[q, pl.ds(pl.multiple_of(src * cap, cap), cap)],
            dst_ref=arr.at[q, pl.ds(pl.multiple_of(src * cap, cap), cap)],
            send_sem=a_send.at[q, 0],
            recv_sem=a_recv.at[q, src],
            device_id=(t, src),
            device_id_type=MESH,
        )

    def exchange(q):
        def body(d, _):
            a_copy(q, d).start()
            return 0

        lax.fori_loop(1, n_sn, body, 0)
        own = pl.ds(pl.multiple_of(s * cap, cap), cap)
        arr[q, own] = sendb[q, own]

    loads[2].wait()
    pick(0)
    pl.semaphore_wait(barrier, n_greet + jnp.where(t > 0, 1, 0) + jnp.where(t < n_tm - 1, 1, 0))
    exchange(0)
    exchange(1)
    loads[3].wait()
    pick(1)
    exchange(2)
    exchange(3)

    loads[1].wait()
    lane_rows = lax.broadcasted_iota(jnp.int32, (cap, sd), 1).astype(F32)
    for o in range(n_sn):
        hit = jnp.where(column(rowv, o) == lane_rows, 1.0, 0.0).astype(BF16)
        one[o * cap : (o + 1) * cap, :sd] = hit
    put[...] = jnp.transpose(one[: n_sn * cap, :sd])

    loads[4].wait()
    for i in range(8):
        cols = pl.ds(LANES * i, LANES)
        if i > 0:
            big[: INPUTS * i, cols] = jnp.zeros((INPUTS * i, LANES), BF16)
        big[INPUTS * i : INPUTS * i + span, cols] = sk[...]
        big[INPUTS * i + span :, cols] = jnp.zeros((LANES - INPUTS * i, LANES), BF16)

    @pl.when(t >= n_tm - 2)
    def _():
        hx[8:12] = jnp.zeros((4, sd, LANES), BF16)
        ht[8 * LANES :, :] = jnp.zeros((4 * LANES, sd), BF16)

    @pl.when(t == n_tm - 1)
    def _():
        hx[4:8] = jnp.zeros((4, sd, LANES), BF16)
        ht[4 * LANES : 8 * LANES, :] = jnp.zeros((4 * LANES, sd), BF16)

    def h_copy(c):
        return pltpu.make_async_remote_copy(
            src_ref=hx.at[c],
            dst_ref=hx.at[c + 4],
            send_sem=h_send.at[c],
            recv_sem=h_recv.at[c],
            device_id=(jnp.maximum(t - 1, 0), s),
            device_id_type=MESH,
        )

    def turn(c):
        ht[LANES * c : LANES * (c + 1), :] = jnp.transpose(hx[c])

    def place(q):
        def body(d, _):
            a_arrival(q, lax.rem(s + d, n_sn)).wait_recv()
            return 0

        lax.fori_loop(1, n_sn, body, 0)
        hx[q] = dot(put[...], arr[q]).astype(BF16)

        @pl.when(t > 0)
        def _():
            h_copy(q).start()

        turn(q)

    def relay(q):
        @pl.when(t < n_tm - 1)
        def _():
            h_copy(q).wait_recv()

            @pl.when(t > 0)
            def _():
                h_copy(4 + q).start()

            turn(4 + q)

    def part(u, chunks, first):
        lhs = jnp.concatenate([hx[c] for c in chunks], axis=1)
        low = LANES * (chunks[0] - u)
        for v in range(4):
            r = dot(lhs, big[low : low + LANES * len(chunks), 256 * v : 256 * v + 256])
            for i in range(2):
                piece = r[:, LANES * i : LANES * (i + 1)]
                hb[u, 2 * v + i] = piece if first else hb[u, 2 * v + i] + piece

    place(0)
    place(1)
    relay(0)
    place(2)
    relay(1)
    place(3)
    for u in range(4):
        part(u, list(range(u, 4)), True)
    relay(2)
    relay(3)
    for u in range(4):
        part(u, [4, 5, 6, 7], False)

    def out_copy(u):
        return pltpu.make_async_copy(hb.at[u], hank.at[pl.ds(8 * u, 8)], out_sem.at[u])

    for u in range(4):
        @pl.when(t < n_tm - 2)
        def _():
            h_copy(4 + u).wait_recv()
            turn(8 + u)

        chunks = list(range(8, 9 + u))
        lhs = jnp.concatenate([hx[c] for c in chunks], axis=1)
        low = LANES * (8 - u)
        for v in range(4):
            r = dot(lhs, big[low : low + LANES * len(chunks), 256 * v : 256 * v + 256])
            r = r + jnp.concatenate([hb[u, 2 * v], hb[u, 2 * v + 1]], axis=1)
            hb[u, 2 * v] = r[:, :LANES]
            hb[u, 2 * v + 1] = r[:, LANES:]
            rb[v * sd : (v + 1) * sd, :] = r.astype(BF16)
        out_copy(u).start()
        rows = span + INPUTS
        lhs = jnp.concatenate([ht[LANES * u + 32 * v : LANES * u + 32 * v + rows, :] for v in range(4)], axis=1)
        grown = dot(lhs, rb[...])
        acc2[...] = grown if u == 0 else acc2[...] + grown

    tr = tot.shape[3]
    whole = acc2[:span, :LANES] + acc2[INPUTS : INPUTS + span, LANES:]
    tot[...] = whole.reshape(tot.shape)

    def s0_copy(a):
        return pltpu.make_async_remote_copy(
            src_ref=tot.at[a, pl.ds((1 - k) * zh, zh)],
            dst_ref=s0b.at[a],
            send_sem=s0_send.at[a],
            recv_sem=s0_recv.at[a],
            device_id=(t, s + 1 - 2 * k),
            device_id_type=MESH,
        )

    for a in range(n_xl):
        s0_copy(a).start()

    me = xl * n_xy + xy

    def s1_copy(a, b):
        return pltpu.make_async_remote_copy(
            src_ref=mid.at[a, b],
            dst_ref=s1b.at[me],
            send_sem=s1_send.at[a, b],
            recv_sem=s1_recv.at[me],
            device_id=(a * n_z + z, b * 2 + k),
            device_id_type=MESH,
        )

    def s1_arrival(e):
        return pltpu.make_async_remote_copy(
            src_ref=mid.at[0, 0],
            dst_ref=s1b.at[e],
            send_sem=s1_send.at[0, 0],
            recv_sem=s1_recv.at[e],
            device_id=(t, s),
            device_id_type=MESH,
        )

    for a in range(n_xl):
        s0_copy(a).wait_recv()
        for c in range(zh):
            mid[a, :, c] = tot[a, k * zh + c] + s0b[a, c]

        def body(d, _):
            b = lax.rem(xy + d, n_xy)

            @pl.when((a != xl) | (b != xy))
            def _():
                s1_copy(a, b).start()

            return 0

        lax.fori_loop(0, n_xy, body, 0)

    s1b[me] = mid[xl, xy]

    def s1_wait(d, _):
        s1_arrival(lax.rem(me + d, n_xl * n_xy)).wait_recv()
        return 0

    lax.fori_loop(1, n_xl * n_xy, s1_wait, 0)
    m2[...] = jnp.sum(s1b[...], axis=0)

    def s2_copy(c, kk):
        return pltpu.make_async_remote_copy(
            src_ref=m2.at[c],
            dst_ref=s2b.at[z],
            send_sem=s2_send.at[c, kk],
            recv_sem=s2_recv.at[z],
            device_id=(xl * n_z + k * zh + c, s - k + kk),
            device_id_type=MESH,
        )

    def s2_arrival(e):
        return pltpu.make_async_remote_copy(
            src_ref=m2.at[0],
            dst_ref=s2b.at[e],
            send_sem=s2_send.at[0, 0],
            recv_sem=s2_recv.at[e],
            device_id=(t, s),
            device_id_type=MESH,
        )

    for c in range(zh):
        for kk in range(2):
            @pl.when((k * zh + c != z) | (k != kk))
            def _():
                s2_copy(c, kk).start()

    @pl.when(z // zh == k)
    def _():
        s2b[z] = m2[z - k * zh]

    for e in range(n_z):
        @pl.when((e != z) | (z // zh != k))
        def _():
            s2_arrival(e).wait_recv()

    done = jnp.sum(s2b[...], axis=0)
    half = tr // 2
    col[...] = jnp.where(k == 0, done[:half], done[half:]) * scale

    for u in range(4):
        out_copy(u).wait()
    for q in range(4):
        def body(d, _):
            a_copy(q, d).wait_send()
            return 0

        lax.fori_loop(1, n_sn, body, 0)

    @pl.when(t > 0)
    def _():
        for q in range(4):
            h_copy(q).wait_send()

    @pl.when((t > 0) & (t < n_tm - 1))
    def _():
        for q in range(4):
            h_copy(4 + q).wait_send()

    for a in range(n_xl):
        s0_copy(a).wait_send()

        def body(b, _):
            @pl.when((a != xl) | (b != xy))
            def _():
                s1_copy(a, b).wait_send()

            return 0

        lax.fori_loop(0, n_xy, body, 0)
    for c in range(zh):
        for kk in range(2):
            @pl.when((k * zh + c != z) | (k != kk))
            def _():
                s2_copy(c, kk).wait_send()


def solution(mesh):
    n_tm, n_sn = mesh.shape["tm"], mesh.shape["sensor"]
    n_xl = 2
    n_z = n_tm // n_xl
    n_xy = n_sn // 2

    def local(state, sketch, cell, row):
        cells, width = state.shape
        span, cols = sketch.shape
        cap = cell.shape[2]
        sd = n_sn * cap // 2
        steps = width // INPUTS
        slots = n_sn * cap
        own_rows = span // (n_tm * n_sn)
        tr = 2 * own_rows
        zh = n_z // 2
        scale = 1.0 / math.sqrt(sd * n_sn * steps * n_tm)
        hbm = pl.BlockSpec(memory_space=pltpu.HBM)
        dma = pltpu.SemaphoreType.DMA
        return pl.pallas_call(
            functools.partial(kernel, n_tm, n_sn, n_xl, 1, scale),
            out_shape=(
                jax.ShapeDtypeStruct((steps, sd, cols), F32),
                jax.ShapeDtypeStruct((own_rows, cols), F32),
            ),
            in_specs=[hbm] * 4,
            out_specs=(hbm, pl.BlockSpec(memory_space=pltpu.VMEM)),
            scratch_shapes=[
                pltpu.VMEM((cells, width), BF16),
                pltpu.VMEM((span, cols), BF16),
                pltpu.VMEM(cell.shape, jnp.int32),
                pltpu.VMEM(row.shape, jnp.int32),
                pltpu.VMEM((slots, cells), BF16),
                pltpu.VMEM((sd, slots), BF16),
                pltpu.VMEM((4, slots, LANES), BF16),
                pltpu.VMEM((4, slots, LANES), BF16),
                pltpu.VMEM((12, sd, LANES), BF16),
                pltpu.VMEM((12 * LANES, sd), BF16),
                pltpu.VMEM((span + LANES, 8 * LANES), BF16),
                pltpu.VMEM((4, 8, sd, LANES), F32),
                pltpu.VMEM((4 * sd, 2 * LANES), BF16),
                pltpu.VMEM((span + INPUTS, 2 * LANES), F32),
                pltpu.VMEM((n_xl, n_z, n_xy, tr, LANES), F32),
                pltpu.VMEM((n_xl, zh, n_xy, tr, LANES), F32),
                pltpu.VMEM((n_xl, n_xy, zh, tr, LANES), F32),
                pltpu.VMEM((n_xl * n_xy, zh, tr, LANES), F32),
                pltpu.VMEM((zh, tr, LANES), F32),
                pltpu.VMEM((n_z, tr, LANES), F32),
                dma((5,)),
                dma((4, n_sn)),
                dma((4, n_sn)),
                dma((8,)),
                dma((8,)),
                dma((4,)),
                dma((n_xl,)),
                dma((n_xl,)),
                dma((n_xl, n_xy)),
                dma((n_xl * n_xy,)),
                dma((zh, 2)),
                dma((n_z,)),
            ],
            compiler_params=pltpu.CompilerParams(
                collective_id=0, has_side_effects=True, vmem_limit_bytes=63 * 2**20
            ),
        )(state, sketch, cell, row)

    placed = (P("sensor", "tm"), P(), P("sensor", None, None), P("sensor", None, None))
    return jax.shard_map(
        local,
        mesh=mesh,
        in_specs=placed,
        out_specs=(P("tm", "sensor", None), P(("tm", "sensor"), None)),
        check_vma=False,
    )
```

```python
import functools
import math

import jax
import jax.numpy as jnp
from jax import lax
from jax.experimental import pallas as pl
from jax.experimental.pallas import tpu as pltpu
from jax.sharding import PartitionSpec as P

INPUTS = 16
KC = 64
LANES = 128
MESH = pl.DeviceIdType.MESH
F32 = jnp.float32
BF16 = jnp.bfloat16


def dot(a, b):
    return jnp.dot(a, b, preferred_element_type=F32)


def kernel(
    n_tm, n_sn, n_xl, n_xh, scale,
    state, sketch, cell, row, hank, col,
    st, sk, cellv, rowv, one, put, sendb, arr, hx, ht, big, hb, rb, acc2, tot, s0b, mid, s1b, m2, s2b,
    ld_sem, a_send, a_recv, h_send, h_recv, out_sem, s0_send, s0_recv, s1_send, s1_recv, s2_send, s2_recv,
):
    t = lax.axis_index("tm")
    s = lax.axis_index("sensor")
    n_z = n_tm // n_xl
    n_xy = n_sn // 2
    zh = n_z // 2
    xl = t // n_z
    z = lax.rem(t, n_z)
    xy = s // 2
    k = lax.rem(s, 2)
    cap = cellv.shape[2]
    sd = hx.shape[1]
    span = sk.shape[0]
    cells = st.shape[0]

    loads = [
        pltpu.make_async_copy(cell, cellv, ld_sem.at[0]),
        pltpu.make_async_copy(row, rowv, ld_sem.at[1]),
        pltpu.make_async_copy(state.at[:, pl.ds(0, 256)], st.at[:, pl.ds(0, 256)], ld_sem.at[2]),
        pltpu.make_async_copy(state.at[:, pl.ds(256, 256)], st.at[:, pl.ds(256, 256)], ld_sem.at[3]),
        pltpu.make_async_copy(sketch, sk, ld_sem.at[4]),
    ]
    for c in loads:
        c.start()

    barrier = pltpu.get_barrier_semaphore()

    def greet(tt, ss):
        pl.semaphore_signal(barrier, inc=1, device_id=(tt, ss), device_id_type=MESH)

    def greet_line(d, _):
        greet(xl * n_z + lax.rem(z + d, n_z), 2 * xy + z // zh)
        return 0

    def greet_sensor(d, _):
        greet(t, lax.rem(s + d, n_sn))
        return 0

    def greet_plane(b, _):
        greet(lax.rem(t + n_z, n_tm), 2 * b + k)
        return 0

    lax.fori_loop(1, n_sn, greet_sensor, 0)
    lax.fori_loop(1, n_z, greet_line, 0)
    lax.fori_loop(0, n_xy, greet_plane, 0)

    @pl.when(t < n_tm - 1)
    def _():
        greet(t + 1, s)

    n_greet = n_sn - 1 + n_xy + 2 * zh - jnp.where(z // zh == k, 2, 0) + jnp.where(t > 0, 1, 0)

    loads[0].wait()
    eye = lax.broadcasted_iota(jnp.int32, (cap, cap), 0) == lax.broadcasted_iota(jnp.int32, (cap, cap), 1)

    def column(ref, o):
        line = ref[0, o : o + 1, :].astype(F32)
        return jnp.sum(jnp.where(eye, jnp.broadcast_to(line, (cap, cap)), 0.0), axis=1, keepdims=True)

    lane_cells = lax.broadcasted_iota(jnp.int32, (cap, cells), 1).astype(F32)
    for o in range(n_sn):
        one[o * cap : (o + 1) * cap, :] = jnp.where(column(cellv, o) == lane_cells, 1.0, 0.0).astype(BF16)

    def pick(half):
        res = dot(one[...], st[:, 256 * half : 256 * half + 256]).astype(BF16)
        sendb[2 * half] = res[:, :LANES]
        sendb[2 * half + 1] = res[:, LANES:]

    def a_copy(q, d):
        dst = lax.rem(s + d, n_sn)
        return pltpu.make_async_remote_copy(
            src_ref=sendb.at[q, pl.ds(pl.multiple_of(dst * cap, cap), cap)],
            dst_ref=arr.at[q, pl.ds(pl.multiple_of(s * cap, cap), cap)],
            send_sem=a_send.at[q, d],
            recv_sem=a_recv.at[q, s],
            device_id=(t, dst),
            device_id_type=MESH,
        )

    def a_arrival(q, src):
        return pltpu.make_async_remote_copy(
            src_ref=sendb.at[q, pl.ds(pl.multiple_of(src * cap, cap), cap)],
            dst_ref=arr.at[q, pl.ds(pl.multiple_of(src * cap, cap), cap)],
            send_sem=a_send.at[q, 0],
            recv_sem=a_recv.at[q, src],
            device_id=(t, src),
            device_id_type=MESH,
        )

    def exchange(q):
        for d in sorted(range(1, n_sn), key=lambda d: (-min(d // 2 % 4, 4 - d // 2 % 4), d)):
            a_copy(q, d).start()
        own = pl.ds(pl.multiple_of(s * cap, cap), cap)
        arr[q, own] = sendb[q, own]

    loads[2].wait()
    pick(0)
    pl.semaphore_wait(barrier, n_greet)
    exchange(0)
    exchange(1)
    loads[3].wait()
    pick(1)
    exchange(2)
    exchange(3)

    loads[1].wait()
    lane_rows = lax.broadcasted_iota(jnp.int32, (cap, sd), 1).astype(F32)
    for o in range(n_sn):
        hit = jnp.where(column(rowv, o) == lane_rows, 1.0, 0.0).astype(BF16)
        one[o * cap : (o + 1) * cap, :sd] = hit
    put[...] = jnp.transpose(one[: n_sn * cap, :sd])

    loads[4].wait()
    for i in range(8):
        cols = pl.ds(LANES * i, LANES)
        if i > 0:
            big[: INPUTS * i, cols] = jnp.zeros((INPUTS * i, LANES), BF16)
        big[INPUTS * i : INPUTS * i + span, cols] = sk[...]
        big[INPUTS * i + span :, cols] = jnp.zeros((LANES - INPUTS * i, LANES), BF16)

    @pl.when(t >= n_tm - 2)
    def _():
        hx[8:12] = jnp.zeros((4, sd, LANES), BF16)
        ht[8 * LANES :, :] = jnp.zeros((4 * LANES, sd), BF16)

    @pl.when(t == n_tm - 1)
    def _():
        hx[4:8] = jnp.zeros((4, sd, LANES), BF16)
        ht[4 * LANES : 8 * LANES, :] = jnp.zeros((4 * LANES, sd), BF16)

    def h_copy(c):
        return pltpu.make_async_remote_copy(
            src_ref=hx.at[c],
            dst_ref=hx.at[c + 4],
            send_sem=h_send.at[c],
            recv_sem=h_recv.at[c],
            device_id=(jnp.maximum(t - 1, 0), s),
            device_id_type=MESH,
        )

    def turn(c):
        ht[LANES * c : LANES * (c + 1), :] = jnp.transpose(hx[c])

    def place(q):
        def body(d, _):
            a_arrival(q, lax.rem(s + d, n_sn)).wait_recv()
            return 0

        lax.fori_loop(1, n_sn, body, 0)
        hx[q] = dot(put[...], arr[q]).astype(BF16)

        @pl.when(t > 0)
        def _():
            h_copy(q).start()

        turn(q)

    def relay(q):
        @pl.when(t < n_tm - 1)
        def _():
            h_copy(q).wait_recv()

            @pl.when(t > 0)
            def _():
                h_copy(4 + q).start()

            turn(4 + q)

    def part(u, chunks, first):
        lhs = jnp.concatenate([hx[c] for c in chunks], axis=1)
        low = LANES * (chunks[0] - u)
        for v in range(4):
            r = dot(lhs, big[low : low + LANES * len(chunks), 256 * v : 256 * v + 256])
            for i in range(2):
                piece = r[:, LANES * i : LANES * (i + 1)]
                hb[u, 2 * v + i] = piece if first else hb[u, 2 * v + i] + piece

    place(0)
    place(1)
    part(0, [0, 1], True)
    part(1, [1], True)
    relay(0)
    place(2)
    relay(1)
    place(3)
    part(0, [2, 3], False)
    part(1, [2, 3], False)
    relay(2)
    part(2, [2, 3], True)
    part(3, [3], True)
    for u in range(4):
        part(u, [4, 5], False)
    relay(3)
    for u in range(4):
        part(u, [6, 7], False)

    def out_copy(u):
        return pltpu.make_async_copy(hb.at[u], hank.at[pl.ds(8 * u, 8)], out_sem.at[u])

    def s0_copy(a):
        return pltpu.make_async_remote_copy(
            src_ref=tot.at[a, pl.ds((1 - k) * zh, zh)],
            dst_ref=s0b.at[a],
            send_sem=s0_send.at[a],
            recv_sem=s0_recv.at[a],
            device_id=(t, s + 1 - 2 * k),
            device_id_type=MESH,
        )

    def image(u, low, high):
        lhs = jnp.concatenate(
            [ht[LANES * u + 32 * v + low : LANES * u + 32 * v + high, :] for v in range(4)], axis=1
        )
        new = dot(lhs, rb[...])
        acc2[low:high, :] = new if u == 0 else acc2[low:high, :] + new

    half_span = span // n_xl

    def grow(u):
        if u < 3:
            image(u, 0, span + INPUTS)
            return
        for a in range(n_xl):
            low = half_span * a
            image(u, low + INPUTS if a else 0, low + half_span + INPUTS)
            whole = acc2[low : low + half_span, :LANES]
            whole = whole + acc2[low + INPUTS : low + half_span + INPUTS, LANES:]
            tot[a] = whole.reshape(tot.shape[1:])
            s0_copy(a).start()

    for u in range(4):
        @pl.when(t < n_tm - 2)
        def _():
            h_copy(4 + u).wait_recv()
            turn(8 + u)

        chunks = list(range(8, 9 + u))
        lhs = jnp.concatenate([hx[c] for c in chunks], axis=1)
        low = LANES * (8 - u)
        for v in range(4):
            r = dot(lhs, big[low : low + LANES * len(chunks), 256 * v : 256 * v + 256])
            r = r + jnp.concatenate([hb[u, 2 * v], hb[u, 2 * v + 1]], axis=1)
            hb[u, 2 * v] = r[:, :LANES]
            hb[u, 2 * v + 1] = r[:, LANES:]
            rb[v * sd : (v + 1) * sd, :] = r.astype(BF16)
        out_copy(u).start()
        grow(u)

    me = xl * n_xy + xy

    def s1_copy(a, b):
        return pltpu.make_async_remote_copy(
            src_ref=mid.at[a, b],
            dst_ref=s1b.at[me],
            send_sem=s1_send.at[a, b],
            recv_sem=s1_recv.at[me],
            device_id=(a * n_z + z, b * 2 + k),
            device_id_type=MESH,
        )

    def s1_arrival(e):
        return pltpu.make_async_remote_copy(
            src_ref=mid.at[0, 0],
            dst_ref=s1b.at[e],
            send_sem=s1_send.at[0, 0],
            recv_sem=s1_recv.at[e],
            device_id=(t, s),
            device_id_type=MESH,
        )

    for a in range(n_xl):
        s0_copy(a).wait_recv()
        for c in range(zh):
            mid[a, :, c] = tot[a, k * zh + c] + s0b[a, c]

        for d in sorted(range(n_xy), key=lambda d: -min(d % 4, 4 - d % 4)):
            b = lax.rem(xy + d, n_xy)
            if d:
                s1_copy(a, b).start()
            else:
                @pl.when(a != xl)
                def _():
                    s1_copy(a, b).start()


    s1b[me] = mid[xl, xy]

    def s1_wait(d, _):
        s1_arrival(lax.rem(me + d, n_xl * n_xy)).wait_recv()
        return 0

    lax.fori_loop(1, n_xl * n_xy, s1_wait, 0)
    m2[...] = jnp.sum(s1b[...], axis=0)

    def s2_copy(c, kk):
        return pltpu.make_async_remote_copy(
            src_ref=m2.at[c],
            dst_ref=s2b.at[z],
            send_sem=s2_send.at[c, kk],
            recv_sem=s2_recv.at[z],
            device_id=(xl * n_z + k * zh + c, s - k + kk),
            device_id_type=MESH,
        )

    def s2_arrival(e):
        return pltpu.make_async_remote_copy(
            src_ref=m2.at[0],
            dst_ref=s2b.at[e],
            send_sem=s2_send.at[0, 0],
            recv_sem=s2_recv.at[e],
            device_id=(t, s),
            device_id_type=MESH,
        )

    for c in range(zh):
        for kk in range(2):
            @pl.when((k * zh + c != z) | (k != kk))
            def _():
                s2_copy(c, kk).start()

    @pl.when(z // zh == k)
    def _():
        s2b[z] = m2[z - k * zh]

    for e in range(n_z):
        @pl.when((e != z) | (z // zh != k))
        def _():
            s2_arrival(e).wait_recv()

    done = jnp.sum(s2b[...], axis=0)
    half = tot.shape[3] // 2
    col[...] = jnp.where(k == 0, done[:half], done[half:]) * scale

    for u in range(4):
        out_copy(u).wait()
    for q in range(4):
        def body(d, _):
            a_copy(q, d).wait_send()
            return 0

        lax.fori_loop(1, n_sn, body, 0)

    @pl.when(t > 0)
    def _():
        for q in range(4):
            h_copy(q).wait_send()

    @pl.when((t > 0) & (t < n_tm - 1))
    def _():
        for q in range(4):
            h_copy(4 + q).wait_send()

    for a in range(n_xl):
        s0_copy(a).wait_send()

        def body(b, _):
            @pl.when((a != xl) | (b != xy))
            def _():
                s1_copy(a, b).wait_send()

            return 0

        lax.fori_loop(0, n_xy, body, 0)
    for c in range(zh):
        for kk in range(2):
            @pl.when((k * zh + c != z) | (k != kk))
            def _():
                s2_copy(c, kk).wait_send()


def flush(hank, col, hank_out, col_out, sems):
    copies = [pltpu.make_async_copy(col, col_out, sems.at[0])]
    for u in range(4):
        part = pl.ds(8 * u, 8)
        copies.append(pltpu.make_async_copy(hank.at[part], hank_out.at[part], sems.at[1 + u]))
    for c in copies:
        c.start()
    for c in copies:
        c.wait()


def solution(mesh):
    n_tm, n_sn = mesh.shape["tm"], mesh.shape["sensor"]
    n_xl = 2
    n_z = n_tm // n_xl
    n_xy = n_sn // 2

    def local(state, sketch, cell, row):
        cells, width = state.shape
        span, cols = sketch.shape
        cap = cell.shape[2]
        sd = n_sn * cap // 2
        steps = width // INPUTS
        slots = n_sn * cap
        own_rows = span // (n_tm * n_sn)
        tr = 2 * own_rows
        zh = n_z // 2
        scale = 1.0 / math.sqrt(sd * n_sn * steps * n_tm)
        hbm = pl.BlockSpec(memory_space=pl.ANY)
        dma = pltpu.SemaphoreType.DMA
        hank, col = pl.pallas_call(
            functools.partial(kernel, n_tm, n_sn, n_xl, 1, scale),
            out_shape=(
                jax.ShapeDtypeStruct((steps, sd, cols), F32),
                jax.ShapeDtypeStruct((own_rows, cols), F32),
            ),
            in_specs=[hbm] * 4,
            out_specs=(hbm, pl.BlockSpec(memory_space=pltpu.VMEM)),
            scratch_shapes=[
                pltpu.VMEM((cells, width), BF16),
                pltpu.VMEM((span, cols), BF16),
                pltpu.VMEM(cell.shape, jnp.int32),
                pltpu.VMEM(row.shape, jnp.int32),
                pltpu.VMEM((slots, cells), BF16),
                pltpu.VMEM((sd, slots), BF16),
                pltpu.VMEM((4, slots, LANES), BF16),
                pltpu.VMEM((4, slots, LANES), BF16),
                pltpu.VMEM((12, sd, LANES), BF16),
                pltpu.VMEM((12 * LANES, sd), BF16),
                pltpu.VMEM((span + LANES, 8 * LANES), BF16),
                pltpu.VMEM((4, 8, sd, LANES), F32),
                pltpu.VMEM((4 * sd, 2 * LANES), BF16),
                pltpu.VMEM((span + INPUTS, 2 * LANES), F32),
                pltpu.VMEM((n_xl, n_z, n_xy, tr, LANES), F32),
                pltpu.VMEM((n_xl, zh, n_xy, tr, LANES), F32),
                pltpu.VMEM((n_xl, n_xy, zh, tr, LANES), F32),
                pltpu.VMEM((n_xl * n_xy, zh, tr, LANES), F32),
                pltpu.VMEM((zh, tr, LANES), F32),
                pltpu.VMEM((n_z, tr, LANES), F32),
                dma((5,)),
                dma((4, n_sn)),
                dma((4, n_sn)),
                dma((8,)),
                dma((8,)),
                dma((4,)),
                dma((n_xl,)),
                dma((n_xl,)),
                dma((n_xl, n_xy)),
                dma((n_xl * n_xy,)),
                dma((zh, 2)),
                dma((n_z,)),
            ],
            compiler_params=pltpu.CompilerParams(
                collective_id=0, has_side_effects=True, vmem_limit_bytes=40 * 2**20
            ),
        )(*[pltpu.with_memory_space_constraint(v, pltpu.HBM) for v in (state, sketch, cell, row)])
        return pl.pallas_call(
            flush,
            out_shape=(
                jax.ShapeDtypeStruct(hank.shape, F32),
                jax.ShapeDtypeStruct(col.shape, F32),
            ),
            in_specs=[hbm] * 2,
            out_specs=(hbm, hbm),
            scratch_shapes=[dma((5,))],
            compiler_params=pltpu.CompilerParams(vmem_limit_bytes=2**20),
        )(hank, col)

    placed = (P("sensor", "tm"), P(), P("sensor", None, None), P("sensor", None, None))
    return jax.shard_map(
        local,
        mesh=mesh,
        in_specs=placed,
        out_specs=(P("tm", "sensor", None), P(("tm", "sensor"), None)),
        check_vma=False,
    )
```

```python
import functools
import math

import jax
import jax.numpy as jnp
from jax import lax
from jax.experimental import pallas as pl
from jax.experimental.pallas import tpu as pltpu
from jax.sharding import PartitionSpec as P

INPUTS = 16
KC = 64
LANES = 128
MESH = pl.DeviceIdType.MESH
F32 = jnp.float32
BF16 = jnp.bfloat16


def dot(a, b):
    return jnp.dot(a, b, preferred_element_type=F32)


def kernel(
    n_tm, n_sn, n_xl, n_xh, scale,
    state, sketch, cell, row, hank, col,
    st, sk, cellv, rowv, one, put, sendb, arr, hx, ht, big, hb, rb, acc2, tot, s0b, mid, s1b, m2, s2b,
    ld_sem, a_send, a_recv, h_send, h_recv, out_sem, s0_send, s0_recv, s1_send, s1_recv, s2_send, s2_recv,
):
    t = lax.axis_index("tm")
    s = lax.axis_index("sensor")
    n_z = n_tm // n_xl
    n_xy = n_sn // 2
    zh = n_z // 2
    xl = t // n_z
    z = lax.rem(t, n_z)
    xy = s // 2
    k = lax.rem(s, 2)
    cap = cellv.shape[2]
    sd = hx.shape[1]
    span = sk.shape[0]
    cells = st.shape[0]

    loads = [
        pltpu.make_async_copy(cell, cellv, ld_sem.at[0]),
        pltpu.make_async_copy(row, rowv, ld_sem.at[1]),
        pltpu.make_async_copy(state.at[:, pl.ds(0, 256)], st.at[:, pl.ds(0, 256)], ld_sem.at[2]),
        pltpu.make_async_copy(state.at[:, pl.ds(256, 256)], st.at[:, pl.ds(256, 256)], ld_sem.at[3]),
        pltpu.make_async_copy(sketch, sk, ld_sem.at[4]),
    ]
    for c in loads:
        c.start()

    barrier = pltpu.get_barrier_semaphore()

    def greet(tt, ss):
        pl.semaphore_signal(barrier, inc=1, device_id=(tt, ss), device_id_type=MESH)

    def greet_line(d, _):
        greet(xl * n_z + lax.rem(z + d, n_z), 2 * xy + z // zh)
        return 0

    def greet_sensor(d, _):
        greet(t, lax.rem(s + d, n_sn))
        return 0

    def greet_plane(b, _):
        greet(lax.rem(t + n_z, n_tm), 2 * b + k)
        return 0

    lax.fori_loop(1, n_sn, greet_sensor, 0)
    lax.fori_loop(1, n_z, greet_line, 0)
    lax.fori_loop(0, n_xy, greet_plane, 0)

    @pl.when(t < n_tm - 1)
    def _():
        greet(t + 1, s)

    n_greet = n_sn - 1 + n_xy + 2 * zh - jnp.where(z // zh == k, 2, 0) + jnp.where(t > 0, 1, 0)

    loads[0].wait()
    eye = lax.broadcasted_iota(jnp.int32, (cap, cap), 0) == lax.broadcasted_iota(jnp.int32, (cap, cap), 1)

    def column(ref, o):
        line = ref[0, o : o + 1, :].astype(F32)
        return jnp.sum(jnp.where(eye, jnp.broadcast_to(line, (cap, cap)), 0.0), axis=1, keepdims=True)

    lane_cells = lax.broadcasted_iota(jnp.int32, (cap, cells), 1).astype(F32)
    for o in range(n_sn):
        one[o * cap : (o + 1) * cap, :] = jnp.where(column(cellv, o) == lane_cells, 1.0, 0.0).astype(BF16)

    def pick(half):
        res = dot(one[...], st[:, 256 * half : 256 * half + 256]).astype(BF16)
        sendb[2 * half] = res[:, :LANES]
        sendb[2 * half + 1] = res[:, LANES:]

    def a_copy(q, d):
        dst = lax.rem(s + d, n_sn)
        return pltpu.make_async_remote_copy(
            src_ref=sendb.at[q, pl.ds(pl.multiple_of(dst * cap, cap), cap)],
            dst_ref=arr.at[q, pl.ds(pl.multiple_of(s * cap, cap), cap)],
            send_sem=a_send.at[q, d],
            recv_sem=a_recv.at[q, s],
            device_id=(t, dst),
            device_id_type=MESH,
        )

    def a_arrival(q, src):
        return pltpu.make_async_remote_copy(
            src_ref=sendb.at[q, pl.ds(pl.multiple_of(src * cap, cap), cap)],
            dst_ref=arr.at[q, pl.ds(pl.multiple_of(src * cap, cap), cap)],
            send_sem=a_send.at[q, 0],
            recv_sem=a_recv.at[q, src],
            device_id=(t, src),
            device_id_type=MESH,
        )

    def exchange(q):
        for d in sorted(range(1, n_sn), key=lambda d: (-min(d // 2 % 4, 4 - d // 2 % 4), d)):
            a_copy(q, d).start()
        own = pl.ds(pl.multiple_of(s * cap, cap), cap)
        arr[q, own] = sendb[q, own]

    loads[2].wait()
    pick(0)
    pl.semaphore_wait(barrier, n_greet)
    exchange(0)
    exchange(1)
    loads[3].wait()
    pick(1)
    exchange(2)
    exchange(3)

    loads[1].wait()
    lane_rows = lax.broadcasted_iota(jnp.int32, (cap, sd), 1).astype(F32)
    for o in range(n_sn):
        hit = jnp.where(column(rowv, o) == lane_rows, 1.0, 0.0).astype(BF16)
        one[o * cap : (o + 1) * cap, :sd] = hit
    put[...] = jnp.transpose(one[: n_sn * cap, :sd])

    loads[4].wait()
    for i in range(8):
        cols = pl.ds(LANES * i, LANES)
        if i > 0:
            big[: INPUTS * i, cols] = jnp.zeros((INPUTS * i, LANES), BF16)
        big[INPUTS * i : INPUTS * i + span, cols] = sk[...]
        big[INPUTS * i + span :, cols] = jnp.zeros((LANES - INPUTS * i, LANES), BF16)

    @pl.when(t >= n_tm - 2)
    def _():
        hx[8:12] = jnp.zeros((4, sd, LANES), BF16)
        ht[8 * LANES :, :] = jnp.zeros((4 * LANES, sd), BF16)

    @pl.when(t == n_tm - 1)
    def _():
        hx[4:8] = jnp.zeros((4, sd, LANES), BF16)
        ht[4 * LANES : 8 * LANES, :] = jnp.zeros((4 * LANES, sd), BF16)

    def h_copy(c):
        return pltpu.make_async_remote_copy(
            src_ref=hx.at[c],
            dst_ref=hx.at[c + 4],
            send_sem=h_send.at[c],
            recv_sem=h_recv.at[c],
            device_id=(jnp.maximum(t - 1, 0), s),
            device_id_type=MESH,
        )

    def turn(c):
        ht[LANES * c : LANES * (c + 1), :] = jnp.transpose(hx[c])

    def place(q):
        def body(d, _):
            a_arrival(q, lax.rem(s + d, n_sn)).wait_recv()
            return 0

        lax.fori_loop(1, n_sn, body, 0)
        hx[q] = dot(put[...], arr[q]).astype(BF16)

        @pl.when(t > 0)
        def _():
            h_copy(q).start()

        turn(q)

    def relay(q):
        @pl.when(t < n_tm - 1)
        def _():
            h_copy(q).wait_recv()

            @pl.when(t > 0)
            def _():
                h_copy(4 + q).start()

            turn(4 + q)

    def part(u, chunks, first):
        lhs = jnp.concatenate([hx[c] for c in chunks], axis=1)
        low = LANES * (chunks[0] - u)
        for v in range(4):
            r = dot(lhs, big[low : low + LANES * len(chunks), 256 * v : 256 * v + 256])
            for i in range(2):
                piece = r[:, LANES * i : LANES * (i + 1)]
                hb[u, 2 * v + i] = piece if first else hb[u, 2 * v + i] + piece

    place(0)
    place(1)
    part(0, [0, 1], True)
    part(1, [1], True)
    place(2)
    place(3)
    relay(0)
    relay(1)
    part(0, [2, 3], False)
    part(1, [2, 3], False)
    part(2, [2, 3], True)
    relay(2)
    part(3, [3], True)
    for u in range(4):
        part(u, [4, 5], False)
    relay(3)
    for u in range(4):
        part(u, [6, 7], False)

    def out_copy(u):
        return pltpu.make_async_copy(hb.at[u], hank.at[pl.ds(8 * u, 8)], out_sem.at[u])

    def s0_copy(a):
        return pltpu.make_async_remote_copy(
            src_ref=tot.at[a, pl.ds((1 - k) * zh, zh)],
            dst_ref=s0b.at[a],
            send_sem=s0_send.at[a],
            recv_sem=s0_recv.at[a],
            device_id=(t, s + 1 - 2 * k),
            device_id_type=MESH,
        )

    def image(u, low, high):
        lhs = jnp.concatenate(
            [ht[LANES * u + 32 * v + low : LANES * u + 32 * v + high, :] for v in range(4)], axis=1
        )
        new = dot(lhs, rb[...])
        acc2[low:high, :] = new if u == 0 else acc2[low:high, :] + new

    half_span = span // n_xl

    def grow(u):
        if u < 3:
            image(u, 0, span + INPUTS)
            return
        for a in range(n_xl):
            low = half_span * a
            image(u, low + INPUTS if a else 0, low + half_span + INPUTS)
            whole = acc2[low : low + half_span, :LANES]
            whole = whole + acc2[low + INPUTS : low + half_span + INPUTS, LANES:]
            tot[a] = whole.reshape(tot.shape[1:])
            s0_copy(a).start()

    for u in range(4):
        @pl.when(t < n_tm - 2)
        def _():
            h_copy(4 + u).wait_recv()
            turn(8 + u)

        chunks = [8 + u] if u % 2 == 0 else [7 + u, 8 + u]
        lhs = jnp.concatenate([hx[c] for c in chunks], axis=1)
        low = LANES * (chunks[0] - u)
        for v in range(4):
            r = dot(lhs, big[low : low + LANES * len(chunks), 256 * v : 256 * v + 256])
            r = r + jnp.concatenate([hb[u, 2 * v], hb[u, 2 * v + 1]], axis=1)
            hb[u, 2 * v] = r[:, :LANES]
            hb[u, 2 * v + 1] = r[:, LANES:]
            rb[v * sd : (v + 1) * sd, :] = r.astype(BF16)
        out_copy(u).start()
        grow(u)
        if u == 1:
            part(2, [8, 9], False)
            part(3, [8, 9], False)

    me = xl * n_xy + xy

    def s1_copy(a, b):
        return pltpu.make_async_remote_copy(
            src_ref=mid.at[a, b],
            dst_ref=s1b.at[me],
            send_sem=s1_send.at[a, b],
            recv_sem=s1_recv.at[me],
            device_id=(a * n_z + z, b * 2 + k),
            device_id_type=MESH,
        )

    def s1_arrival(e):
        return pltpu.make_async_remote_copy(
            src_ref=mid.at[0, 0],
            dst_ref=s1b.at[e],
            send_sem=s1_send.at[0, 0],
            recv_sem=s1_recv.at[e],
            device_id=(t, s),
            device_id_type=MESH,
        )

    for a in range(n_xl):
        s0_copy(a).wait_recv()
        for c in range(zh):
            mid[a, :, c] = tot[a, k * zh + c] + s0b[a, c]

        for d in sorted(range(n_xy), key=lambda d: -min(d % 4, 4 - d % 4)):
            b = lax.rem(xy + d, n_xy)
            if d:
                s1_copy(a, b).start()
            else:
                @pl.when(a != xl)
                def _():
                    s1_copy(a, b).start()


    s1b[me] = mid[xl, xy]

    def s1_wait(d, _):
        s1_arrival(lax.rem(me + d, n_xl * n_xy)).wait_recv()
        return 0

    lax.fori_loop(1, n_xl * n_xy, s1_wait, 0)
    m2[...] = jnp.sum(s1b[...], axis=0)

    def s2_copy(c, kk):
        return pltpu.make_async_remote_copy(
            src_ref=m2.at[c],
            dst_ref=s2b.at[z],
            send_sem=s2_send.at[c, kk],
            recv_sem=s2_recv.at[z],
            device_id=(xl * n_z + k * zh + c, s - k + kk),
            device_id_type=MESH,
        )

    def s2_arrival(e):
        return pltpu.make_async_remote_copy(
            src_ref=m2.at[0],
            dst_ref=s2b.at[e],
            send_sem=s2_send.at[0, 0],
            recv_sem=s2_recv.at[e],
            device_id=(t, s),
            device_id_type=MESH,
        )

    for c in range(zh):
        for kk in range(2):
            @pl.when((k * zh + c != z) | (k != kk))
            def _():
                s2_copy(c, kk).start()

    @pl.when(z // zh == k)
    def _():
        s2b[z] = m2[z - k * zh]

    for e in range(n_z):
        @pl.when((e != z) | (z // zh != k))
        def _():
            s2_arrival(e).wait_recv()

    done = jnp.sum(s2b[...], axis=0)
    half = tot.shape[3] // 2
    col[...] = jnp.where(k == 0, done[:half], done[half:]) * scale

    for u in range(4):
        out_copy(u).wait()
    for q in range(4):
        def body(d, _):
            a_copy(q, d).wait_send()
            return 0

        lax.fori_loop(1, n_sn, body, 0)

    @pl.when(t > 0)
    def _():
        for q in range(4):
            h_copy(q).wait_send()

    @pl.when((t > 0) & (t < n_tm - 1))
    def _():
        for q in range(4):
            h_copy(4 + q).wait_send()

    for a in range(n_xl):
        s0_copy(a).wait_send()

        def body(b, _):
            @pl.when((a != xl) | (b != xy))
            def _():
                s1_copy(a, b).wait_send()

            return 0

        lax.fori_loop(0, n_xy, body, 0)
    for c in range(zh):
        for kk in range(2):
            @pl.when((k * zh + c != z) | (k != kk))
            def _():
                s2_copy(c, kk).wait_send()


def flush(hank, col, hank_out, col_out, sems):
    copies = [pltpu.make_async_copy(col, col_out, sems.at[0])]
    for u in range(16):
        part = pl.ds(2 * u, 2)
        copies.append(pltpu.make_async_copy(hank.at[part], hank_out.at[part], sems.at[1 + u]))
    for c in copies:
        c.start()
    for c in copies:
        c.wait()


def solution(mesh):
    n_tm, n_sn = mesh.shape["tm"], mesh.shape["sensor"]
    n_xl = 2
    n_z = n_tm // n_xl
    n_xy = n_sn // 2

    def local(state, sketch, cell, row):
        cells, width = state.shape
        span, cols = sketch.shape
        cap = cell.shape[2]
        sd = n_sn * cap // 2
        steps = width // INPUTS
        slots = n_sn * cap
        own_rows = span // (n_tm * n_sn)
        tr = 2 * own_rows
        zh = n_z // 2
        scale = 1.0 / math.sqrt(sd * n_sn * steps * n_tm)
        hbm = pl.BlockSpec(memory_space=pl.ANY)
        dma = pltpu.SemaphoreType.DMA
        hank, col = pl.pallas_call(
            functools.partial(kernel, n_tm, n_sn, n_xl, 1, scale),
            out_shape=(
                jax.ShapeDtypeStruct((steps, sd, cols), F32),
                jax.ShapeDtypeStruct((own_rows, cols), F32),
            ),
            in_specs=[hbm] * 4,
            out_specs=(hbm, pl.BlockSpec(memory_space=pltpu.VMEM)),
            scratch_shapes=[
                pltpu.VMEM((cells, width), BF16),
                pltpu.VMEM((span, cols), BF16),
                pltpu.VMEM(cell.shape, jnp.int32),
                pltpu.VMEM(row.shape, jnp.int32),
                pltpu.VMEM((slots, cells), BF16),
                pltpu.VMEM((sd, slots), BF16),
                pltpu.VMEM((4, slots, LANES), BF16),
                pltpu.VMEM((4, slots, LANES), BF16),
                pltpu.VMEM((12, sd, LANES), BF16),
                pltpu.VMEM((12 * LANES, sd), BF16),
                pltpu.VMEM((span + LANES, 8 * LANES), BF16),
                pltpu.VMEM((4, 8, sd, LANES), F32),
                pltpu.VMEM((4 * sd, 2 * LANES), BF16),
                pltpu.VMEM((span + INPUTS, 2 * LANES), F32),
                pltpu.VMEM((n_xl, n_z, n_xy, tr, LANES), F32),
                pltpu.VMEM((n_xl, zh, n_xy, tr, LANES), F32),
                pltpu.VMEM((n_xl, n_xy, zh, tr, LANES), F32),
                pltpu.VMEM((n_xl * n_xy, zh, tr, LANES), F32),
                pltpu.VMEM((zh, tr, LANES), F32),
                pltpu.VMEM((n_z, tr, LANES), F32),
                dma((5,)),
                dma((4, n_sn)),
                dma((4, n_sn)),
                dma((8,)),
                dma((8,)),
                dma((4,)),
                dma((n_xl,)),
                dma((n_xl,)),
                dma((n_xl, n_xy)),
                dma((n_xl * n_xy,)),
                dma((zh, 2)),
                dma((n_z,)),
            ],
            compiler_params=pltpu.CompilerParams(
                collective_id=0, has_side_effects=True, vmem_limit_bytes=40 * 2**20
            ),
        )(*[pltpu.with_memory_space_constraint(v, pltpu.HBM) for v in (state, sketch, cell, row)])
        return pl.pallas_call(
            flush,
            out_shape=(
                jax.ShapeDtypeStruct(hank.shape, F32),
                jax.ShapeDtypeStruct(col.shape, F32),
            ),
            in_specs=[hbm] * 2,
            out_specs=(hbm, hbm),
            scratch_shapes=[dma((17,))],
            compiler_params=pltpu.CompilerParams(vmem_limit_bytes=2**20),
        )(hank, col)

    placed = (P("sensor", "tm"), P(), P("sensor", None, None), P("sensor", None, None))
    return jax.shard_map(
        local,
        mesh=mesh,
        in_specs=placed,
        out_specs=(P("tm", "sensor", None), P(("tm", "sensor"), None)),
        check_vma=False,
    )
```

```python
import functools
import math

import jax
import jax.numpy as jnp
from jax import lax
from jax.experimental import pallas as pl
from jax.experimental.pallas import tpu as pltpu
from jax.sharding import PartitionSpec as P

INPUTS = 16
KC = 64
LANES = 128
MESH = pl.DeviceIdType.MESH
AHEAD = 3
FIRST = 4 - AHEAD
F32 = jnp.float32
BF16 = jnp.bfloat16


def dot(a, b):
    return jnp.dot(a, b, preferred_element_type=F32)


def kernel(
    n_tm, n_sn, n_xl, n_xh, scale,
    state, sketch, cell, row, hank, col,
    st, sk, cellv, rowv, one, put, sendb, arr, hx, ht, big, hb, rb, acc2, tot, s0b, mid, s1b, m2, s2b,
    ld_sem, a_send, a_recv, h_send, h_recv, out_sem, s0_send, s0_recv, s1_send, s1_recv, s2_send, s2_recv,
):
    t = lax.axis_index("tm")
    s = lax.axis_index("sensor")
    n_z = n_tm // n_xl
    n_xy = n_sn // 2
    zh = n_z // 2
    xl = t // n_z
    z = lax.rem(t, n_z)
    xy = s // 2
    k = lax.rem(s, 2)
    cap = cellv.shape[2]
    sd = hx.shape[1]
    span = sk.shape[0]
    cells = st.shape[0]

    loads = [
        pltpu.make_async_copy(cell, cellv, ld_sem.at[0]),
        pltpu.make_async_copy(row, rowv, ld_sem.at[1]),
        pltpu.make_async_copy(state.at[:, pl.ds(0, 256)], st.at[:, pl.ds(0, 256)], ld_sem.at[2]),
        pltpu.make_async_copy(state.at[:, pl.ds(256, 256)], st.at[:, pl.ds(256, 256)], ld_sem.at[3]),
        pltpu.make_async_copy(sketch, sk, ld_sem.at[4]),
    ]
    for c in loads:
        c.start()

    barrier = pltpu.get_barrier_semaphore()

    def greet(tt, ss):
        pl.semaphore_signal(barrier, inc=1, device_id=(tt, ss), device_id_type=MESH)

    def greet_line(d, _):
        greet(xl * n_z + lax.rem(z + d, n_z), 2 * xy + z // zh)
        return 0

    def greet_sensor(d, _):
        greet(t, lax.rem(s + d, n_sn))
        return 0

    def greet_plane(b, _):
        greet(lax.rem(t + n_z, n_tm), 2 * b + k)
        return 0

    lax.fori_loop(1, n_sn, greet_sensor, 0)
    lax.fori_loop(1, n_z, greet_line, 0)
    lax.fori_loop(0, n_xy, greet_plane, 0)

    @pl.when(t < n_tm - 1)
    def _():
        greet(t + 1, s)

    @pl.when(t > 0)
    def _():
        greet(t - 1, s)

    n_greet = n_sn - 1 + n_xy + 2 * zh - jnp.where(z // zh == k, 2, 0)
    n_greet = n_greet + jnp.where(t > 0, 1, 0) + jnp.where(t < n_tm - 1, 1, 0)

    loads[0].wait()
    eye = lax.broadcasted_iota(jnp.int32, (cap, cap), 0) == lax.broadcasted_iota(jnp.int32, (cap, cap), 1)

    def column(ref, o):
        line = ref[0, o : o + 1, :].astype(F32)
        return jnp.sum(jnp.where(eye, jnp.broadcast_to(line, (cap, cap)), 0.0), axis=1, keepdims=True)

    lane_cells = lax.broadcasted_iota(jnp.int32, (cap, cells), 1).astype(F32)
    for o in range(n_sn):
        one[o * cap : (o + 1) * cap, :] = jnp.where(column(cellv, o) == lane_cells, 1.0, 0.0).astype(BF16)

    def pick(half):
        res = dot(one[...], st[:, 256 * half : 256 * half + 256]).astype(BF16)
        sendb[2 * half] = res[:, :LANES]
        sendb[2 * half + 1] = res[:, LANES:]

    def a_copy(q, d):
        dst = lax.rem(s + d, n_sn)
        return pltpu.make_async_remote_copy(
            src_ref=sendb.at[q, pl.ds(pl.multiple_of(dst * cap, cap), cap)],
            dst_ref=arr.at[q, pl.ds(pl.multiple_of(s * cap, cap), cap)],
            send_sem=a_send.at[q, d],
            recv_sem=a_recv.at[q, s],
            device_id=(t, dst),
            device_id_type=MESH,
        )

    def a_arrival(q, src):
        return pltpu.make_async_remote_copy(
            src_ref=sendb.at[q, pl.ds(pl.multiple_of(src * cap, cap), cap)],
            dst_ref=arr.at[q, pl.ds(pl.multiple_of(src * cap, cap), cap)],
            send_sem=a_send.at[q, 0],
            recv_sem=a_recv.at[q, src],
            device_id=(t, src),
            device_id_type=MESH,
        )

    def exchange(q):
        for d in sorted(range(1, n_sn), key=lambda d: (-min(d // 2 % 4, 4 - d // 2 % 4), d)):
            a_copy(q, d).start()
        own = pl.ds(pl.multiple_of(s * cap, cap), cap)
        arr[q, own] = sendb[q, own]

    loads[2].wait()
    pick(0)
    pl.semaphore_wait(barrier, n_greet)
    exchange(0)
    exchange(1)
    loads[3].wait()
    pick(1)
    exchange(2)
    exchange(3)

    loads[1].wait()
    lane_rows = lax.broadcasted_iota(jnp.int32, (cap, sd), 1).astype(F32)
    for o in range(n_sn):
        hit = jnp.where(column(rowv, o) == lane_rows, 1.0, 0.0).astype(BF16)
        one[o * cap : (o + 1) * cap, :sd] = hit
    put[...] = jnp.transpose(one[: n_sn * cap, :sd])

    loads[4].wait()
    for i in range(8):
        cols = pl.ds(LANES * i, LANES)
        if i > 0:
            big[: INPUTS * i, cols] = jnp.zeros((INPUTS * i, LANES), BF16)
        big[INPUTS * i : INPUTS * i + span, cols] = sk[...]
        big[INPUTS * i + span :, cols] = jnp.zeros((LANES - INPUTS * i, LANES), BF16)

    @pl.when(t >= n_tm - 2)
    def _():
        hx[12:16] = jnp.zeros((4, sd, LANES), BF16)
        ht[12 * LANES :, :] = jnp.zeros((4 * LANES, sd), BF16)

    @pl.when(t == n_tm - 1)
    def _():
        hx[8:12] = jnp.zeros((4, sd, LANES), BF16)
        ht[8 * LANES : 12 * LANES, :] = jnp.zeros((4 * LANES, sd), BF16)

    acc2[...] = jnp.zeros_like(acc2)

    def h_copy(src, dst, sem, to):
        return pltpu.make_async_remote_copy(
            src_ref=hx.at[src],
            dst_ref=hx.at[dst],
            send_sem=h_send.at[sem],
            recv_sem=h_recv.at[sem],
            device_id=(to, s),
            device_id_type=MESH,
        )

    before, after = jnp.maximum(t - 1, 0), jnp.minimum(t + 1, n_tm - 1)

    def down(q):
        return h_copy(4 + q, 8 + q, q, before)

    def onward(q):
        return h_copy(8 + q, 12 + q, 4 + q, before)

    def up(q):
        return h_copy(4 + q, q, 8 + q, after)

    def turn(c):
        ht[LANES * c : LANES * (c + 1), :] = jnp.transpose(hx[c])

    def place(q):
        def body(d, _):
            a_arrival(q, lax.rem(s + d, n_sn)).wait_recv()
            return 0

        lax.fori_loop(1, n_sn, body, 0)
        hx[4 + q] = dot(put[...], arr[q]).astype(BF16)

        @pl.when(t > 0)
        def _():
            down(q).start()

        if q >= FIRST:
            @pl.when(t < n_tm - 1)
            def _():
                up(q).start()

        turn(4 + q)

    def relay(q):
        @pl.when(t < n_tm - 1)
        def _():
            down(q).wait_recv()

            @pl.when(t > 0)
            def _():
                onward(q).start()

            turn(8 + q)

    def below(q):
        up(q).wait_recv()
        turn(q)

    def above(q):
        @pl.when(t < n_tm - 2)
        def _():
            onward(q).wait_recv()
            if 12 + q < 16 - AHEAD:
                turn(12 + q)

    def weigh(g, chunks, v):
        lhs = jnp.concatenate([hx[c] for c in chunks], axis=1)
        low = LANES * (chunks[0] - g)
        return dot(lhs, big[low : low + LANES * len(chunks), 256 * v : 256 * v + 256])

    def part(g, chunks, first=False):
        for v in range(4):
            r = weigh(g, chunks, v)
            for i in range(2):
                piece = r[:, LANES * i : LANES * (i + 1)]
                hb[g, 2 * v + i] = piece if first else hb[g, 2 * v + i] + piece

    def last_part(g, chunks, rounded, kept):
        for v in range(4):
            r = weigh(g, chunks, v) + jnp.concatenate([hb[g, 2 * v], hb[g, 2 * v + 1]], axis=1)
            if kept:
                hb[g, 2 * v] = r[:, :LANES]
                hb[g, 2 * v + 1] = r[:, LANES:]
            if rounded:
                rb[v * sd : (v + 1) * sd, :] = r.astype(BF16)

    def out_copy(u):
        return pltpu.make_async_copy(hb.at[4 + u], hank.at[pl.ds(8 * u, 8)], out_sem.at[u])

    def image(g, low, high):
        lhs = jnp.concatenate(
            [ht[LANES * g + 32 * v + low : LANES * g + 32 * v + high, :] for v in range(4)], axis=1
        )
        acc2[low:high, :] = acc2[low:high, :] + dot(lhs, rb[...])

    full = span + INPUTS
    shared = list(range(4, 8 - AHEAD))
    ahead = list(range(FIRST, 4))
    later = list(range(8 - AHEAD, 8))

    place(0)
    place(1)
    for g in ahead + shared[:2]:
        part(g, [4, 5] if g < 5 else [5], True)
    place(2)
    place(3)
    relay(0)
    for g in ahead:
        part(g, [6, 7])
    relay(1)
    for g in shared:
        part(g, [6, 7], g == 6)

    @pl.when(t == n_tm - 1)
    def _():
        for g in later:
            for v in range(4):
                rb[v * sd : (v + 1) * sd, :] = weigh(g, list(range(g, 8)), v).astype(BF16)
            image(g, 0, full)

    for g in ahead + shared:
        if g > 0:
            part(g, [8, 9])
    relay(2)

    @pl.when(t > 0)
    def _():
        for q in range(FIRST, 4):
            below(q)
        for g in ahead[:-1]:
            tail = [c for c in range(8, g + 9) if c > 9 or g == 0]
            if tail:
                part(g, tail)
            last_part(g, list(range(g, 4)), True, False)
            image(g, 0, full)

    relay(3)

    @pl.when(t > 0)
    def _():
        part(3, [10, 11])
        last_part(3, [3], True, False)
        image(3, 0, full)

    half_span = span // n_xl

    def s0_copy(a):
        return pltpu.make_async_remote_copy(
            src_ref=tot.at[a, pl.ds((1 - k) * zh, zh)],
            dst_ref=s0b.at[a],
            send_sem=s0_send.at[a],
            recv_sem=s0_recv.at[a],
            device_id=(t, s + 1 - 2 * k),
            device_id_type=MESH,
        )

    for g in shared:
        part(g, [10, 11])
        above(g - 4)
        last_part(g, [12] if g == 4 else list(range(12, g + 9)), True, True)
        out_copy(g - 4).start()
        if g < shared[-1]:
            image(g, 0, full)
            continue
        for a in range(n_xl):
            low = half_span * a
            image(g, low + INPUTS if a else 0, low + half_span + INPUTS)
            whole = acc2[low : low + half_span, :LANES]
            whole = whole + acc2[low + INPUTS : low + half_span + INPUTS, LANES:]
            tot[a] = whole.reshape(tot.shape[1:])
            s0_copy(a).start()

    for g in later:
        part(g, list(range(g, 8)), True)

    me = xl * n_xy + xy

    def s1_copy(a, b):
        return pltpu.make_async_remote_copy(
            src_ref=mid.at[a, b],
            dst_ref=s1b.at[me],
            send_sem=s1_send.at[a, b],
            recv_sem=s1_recv.at[me],
            device_id=(a * n_z + z, b * 2 + k),
            device_id_type=MESH,
        )

    def s1_arrival(e):
        return pltpu.make_async_remote_copy(
            src_ref=mid.at[0, 0],
            dst_ref=s1b.at[e],
            send_sem=s1_send.at[0, 0],
            recv_sem=s1_recv.at[e],
            device_id=(t, s),
            device_id_type=MESH,
        )

    for a in range(n_xl):
        s0_copy(a).wait_recv()
        for c in range(zh):
            mid[a, :, c] = tot[a, k * zh + c] + s0b[a, c]

        for d in sorted(range(n_xy), key=lambda d: -min(d % 4, 4 - d % 4)):
            b = lax.rem(xy + d, n_xy)
            if d:
                s1_copy(a, b).start()
            else:
                @pl.when(a != xl)
                def _():
                    s1_copy(a, b).start()


    s1b[me] = mid[xl, xy]
    for g in later:
        part(g, [8, 9, 10, 11])

    def s1_wait(d, _):
        s1_arrival(lax.rem(me + d, n_xl * n_xy)).wait_recv()
        return 0

    lax.fori_loop(1, n_xl * n_xy, s1_wait, 0)
    m2[...] = jnp.sum(s1b[...], axis=0)

    def s2_copy(c, kk):
        return pltpu.make_async_remote_copy(
            src_ref=m2.at[c],
            dst_ref=s2b.at[z],
            send_sem=s2_send.at[c, kk],
            recv_sem=s2_recv.at[z],
            device_id=(xl * n_z + k * zh + c, s - k + kk),
            device_id_type=MESH,
        )

    def s2_arrival(e):
        return pltpu.make_async_remote_copy(
            src_ref=m2.at[0],
            dst_ref=s2b.at[e],
            send_sem=s2_send.at[0, 0],
            recv_sem=s2_recv.at[e],
            device_id=(t, s),
            device_id_type=MESH,
        )

    for c in range(zh):
        for kk in range(2):
            @pl.when((k * zh + c != z) | (k != kk))
            def _():
                s2_copy(c, kk).start()

    @pl.when(z // zh == k)
    def _():
        s2b[z] = m2[z - k * zh]

    for g in later:
        above(g - 4)
        last_part(g, list(range(12, g + 9)), False, True)
        out_copy(g - 4).start()

    for e in range(n_z):
        @pl.when((e != z) | (z // zh != k))
        def _():
            s2_arrival(e).wait_recv()

    done = jnp.sum(s2b[...], axis=0)
    half = tot.shape[3] // 2
    col[...] = jnp.where(k == 0, done[:half], done[half:]) * scale

    for u in range(4):
        out_copy(u).wait()
    for q in range(4):
        def body(d, _):
            a_copy(q, d).wait_send()
            return 0

        lax.fori_loop(1, n_sn, body, 0)

    @pl.when(t > 0)
    def _():
        for q in range(4):
            down(q).wait_send()

    @pl.when(t < n_tm - 1)
    def _():
        for q in range(FIRST, 4):
            up(q).wait_send()

        @pl.when(t > 0)
        def _():
            for q in range(4):
                onward(q).wait_send()

    for a in range(n_xl):
        s0_copy(a).wait_send()

        def body(b, _):
            @pl.when((a != xl) | (b != xy))
            def _():
                s1_copy(a, b).wait_send()

            return 0

        lax.fori_loop(0, n_xy, body, 0)
    for c in range(zh):
        for kk in range(2):
            @pl.when((k * zh + c != z) | (k != kk))
            def _():
                s2_copy(c, kk).wait_send()


def flush(hank, col, hank_out, col_out, sems):
    copies = [pltpu.make_async_copy(col, col_out, sems.at[0])]
    for u in range(16):
        part = pl.ds(2 * u, 2)
        copies.append(pltpu.make_async_copy(hank.at[part], hank_out.at[part], sems.at[1 + u]))
    for c in copies:
        c.start()
    for c in copies:
        c.wait()


def solution(mesh):
    n_tm, n_sn = mesh.shape["tm"], mesh.shape["sensor"]
    n_xl = 2
    n_z = n_tm // n_xl
    n_xy = n_sn // 2

    def local(state, sketch, cell, row):
        cells, width = state.shape
        span, cols = sketch.shape
        cap = cell.shape[2]
        sd = n_sn * cap // 2
        steps = width // INPUTS
        slots = n_sn * cap
        own_rows = span // (n_tm * n_sn)
        tr = 2 * own_rows
        zh = n_z // 2
        scale = 1.0 / math.sqrt(sd * n_sn * steps * n_tm)
        hbm = pl.BlockSpec(memory_space=pl.ANY)
        dma = pltpu.SemaphoreType.DMA
        hank, col = pl.pallas_call(
            functools.partial(kernel, n_tm, n_sn, n_xl, 1, scale),
            out_shape=(
                jax.ShapeDtypeStruct((steps, sd, cols), F32),
                jax.ShapeDtypeStruct((own_rows, cols), F32),
            ),
            in_specs=[hbm] * 4,
            out_specs=(hbm, pl.BlockSpec(memory_space=pltpu.VMEM)),
            scratch_shapes=[
                pltpu.VMEM((cells, width), BF16),
                pltpu.VMEM((span, cols), BF16),
                pltpu.VMEM(cell.shape, jnp.int32),
                pltpu.VMEM(row.shape, jnp.int32),
                pltpu.VMEM((slots, cells), BF16),
                pltpu.VMEM((sd, slots), BF16),
                pltpu.VMEM((4, slots, LANES), BF16),
                pltpu.VMEM((4, slots, LANES), BF16),
                pltpu.VMEM((16, sd, LANES), BF16),
                pltpu.VMEM((16 * LANES, sd), BF16),
                pltpu.VMEM((span + LANES, 8 * LANES), BF16),
                pltpu.VMEM((8, 8, sd, LANES), F32),
                pltpu.VMEM((4 * sd, 2 * LANES), BF16),
                pltpu.VMEM((span + INPUTS, 2 * LANES), F32),
                pltpu.VMEM((n_xl, n_z, n_xy, tr, LANES), F32),
                pltpu.VMEM((n_xl, zh, n_xy, tr, LANES), F32),
                pltpu.VMEM((n_xl, n_xy, zh, tr, LANES), F32),
                pltpu.VMEM((n_xl * n_xy, zh, tr, LANES), F32),
                pltpu.VMEM((zh, tr, LANES), F32),
                pltpu.VMEM((n_z, tr, LANES), F32),
                dma((5,)),
                dma((4, n_sn)),
                dma((4, n_sn)),
                dma((12,)),
                dma((12,)),
                dma((4,)),
                dma((n_xl,)),
                dma((n_xl,)),
                dma((n_xl, n_xy)),
                dma((n_xl * n_xy,)),
                dma((zh, 2)),
                dma((n_z,)),
            ],
            compiler_params=pltpu.CompilerParams(
                collective_id=0, has_side_effects=True, vmem_limit_bytes=40 * 2**20
            ),
        )(*[pltpu.with_memory_space_constraint(v, pltpu.HBM) for v in (state, sketch, cell, row)])
        return pl.pallas_call(
            flush,
            out_shape=(
                jax.ShapeDtypeStruct(hank.shape, F32),
                jax.ShapeDtypeStruct(col.shape, F32),
            ),
            in_specs=[hbm] * 2,
            out_specs=(hbm, hbm),
            scratch_shapes=[dma((17,))],
            compiler_params=pltpu.CompilerParams(vmem_limit_bytes=2**20),
        )(hank, col)

    placed = (P("sensor", "tm"), P(), P("sensor", None, None), P("sensor", None, None))
    return jax.shard_map(
        local,
        mesh=mesh,
        in_specs=placed,
        out_specs=(P("tm", "sensor", None), P(("tm", "sensor"), None)),
        check_vma=False,
    )
```

```python
import functools
import math

import jax
import jax.numpy as jnp
from jax import lax
from jax.experimental import pallas as pl
from jax.experimental.pallas import tpu as pltpu
from jax.sharding import PartitionSpec as P

INPUTS = 16
KC = 64
LANES = 128
MESH = pl.DeviceIdType.MESH
AHEAD = 3
FIRST = 4 - AHEAD
F32 = jnp.float32
BF16 = jnp.bfloat16


def dot(a, b):
    return jnp.dot(a, b, preferred_element_type=F32)


def kernel(
    n_tm, n_sn, n_xl, n_xh, scale,
    state, sketch, cell, row, hank, col,
    st, sk, cellv, rowv, one, put, sendb, arr, hx, ht, big, hb, rb, acc2, tot, s0b, mid, s1b, m2, s2b,
    ld_sem, a_send, a_recv, h_send, h_recv, out_sem, s0_send, s0_recv, s1_send, s1_recv, s2_send, s2_recv,
):
    t = lax.axis_index("tm")
    s = lax.axis_index("sensor")
    n_z = n_tm // n_xl
    n_xy = n_sn // 2
    zh = n_z // 2
    xl = t // n_z
    z = lax.rem(t, n_z)
    xy = s // 2
    k = lax.rem(s, 2)
    cap = cellv.shape[2]
    sd = hx.shape[1]
    span = sk.shape[0]
    cells = st.shape[0]

    loads = [
        pltpu.make_async_copy(cell, cellv, ld_sem.at[0]),
        pltpu.make_async_copy(row, rowv, ld_sem.at[1]),
        pltpu.make_async_copy(state.at[:, pl.ds(0, 256)], st.at[:, pl.ds(0, 256)], ld_sem.at[2]),
        pltpu.make_async_copy(state.at[:, pl.ds(256, 256)], st.at[:, pl.ds(256, 256)], ld_sem.at[3]),
        pltpu.make_async_copy(sketch, sk, ld_sem.at[4]),
    ]
    for c in loads:
        c.start()

    barrier = pltpu.get_barrier_semaphore()

    def greet(tt, ss):
        pl.semaphore_signal(barrier, inc=1, device_id=(tt, ss), device_id_type=MESH)

    def greet_line(d, _):
        greet(xl * n_z + lax.rem(z + d, n_z), 2 * xy + z // zh)
        return 0

    def greet_sensor(d, _):
        greet(t, lax.rem(s + d, n_sn))
        return 0

    def greet_plane(b, _):
        greet(lax.rem(t + n_z, n_tm), 2 * b + k)
        return 0

    lax.fori_loop(1, n_sn, greet_sensor, 0)
    lax.fori_loop(1, n_z, greet_line, 0)
    lax.fori_loop(0, n_xy, greet_plane, 0)

    @pl.when(t < n_tm - 1)
    def _():
        greet(t + 1, s)

    @pl.when(t > 0)
    def _():
        greet(t - 1, s)

    n_greet = n_sn - 1 + n_xy + 2 * zh - jnp.where(z // zh == k, 2, 0)
    n_greet = n_greet + jnp.where(t > 0, 1, 0) + jnp.where(t < n_tm - 1, 1, 0)

    loads[0].wait()
    eye = lax.broadcasted_iota(jnp.int32, (cap, cap), 0) == lax.broadcasted_iota(jnp.int32, (cap, cap), 1)

    def column(ref, o):
        line = ref[0, o : o + 1, :].astype(F32)
        return jnp.sum(jnp.where(eye, jnp.broadcast_to(line, (cap, cap)), 0.0), axis=1, keepdims=True)

    lane_cells = lax.broadcasted_iota(jnp.int32, (cap, cells), 1).astype(F32)
    for o in range(n_sn):
        one[o * cap : (o + 1) * cap, :] = jnp.where(column(cellv, o) == lane_cells, 1.0, 0.0).astype(BF16)

    def pick(half):
        res = dot(one[...], st[:, 256 * half : 256 * half + 256]).astype(BF16)
        sendb[2 * half] = res[:, :LANES]
        sendb[2 * half + 1] = res[:, LANES:]

    def a_copy(q, d):
        dst = lax.rem(s + d, n_sn)
        return pltpu.make_async_remote_copy(
            src_ref=sendb.at[q, pl.ds(pl.multiple_of(dst * cap, cap), cap)],
            dst_ref=arr.at[q, pl.ds(pl.multiple_of(s * cap, cap), cap)],
            send_sem=a_send.at[q, d],
            recv_sem=a_recv.at[q, s],
            device_id=(t, dst),
            device_id_type=MESH,
        )

    def a_arrival(q, src):
        return pltpu.make_async_remote_copy(
            src_ref=sendb.at[q, pl.ds(pl.multiple_of(src * cap, cap), cap)],
            dst_ref=arr.at[q, pl.ds(pl.multiple_of(src * cap, cap), cap)],
            send_sem=a_send.at[q, 0],
            recv_sem=a_recv.at[q, src],
            device_id=(t, src),
            device_id_type=MESH,
        )

    def exchange(q):
        for d in sorted(range(1, n_sn), key=lambda d: (-min(d // 2 % 4, 4 - d // 2 % 4), d)):
            a_copy(q, d).start()
        own = pl.ds(pl.multiple_of(s * cap, cap), cap)
        arr[q, own] = sendb[q, own]

    loads[2].wait()
    pick(0)
    pl.semaphore_wait(barrier, n_greet)
    exchange(0)
    exchange(1)
    loads[3].wait()
    pick(1)
    exchange(2)
    exchange(3)

    loads[1].wait()
    lane_rows = lax.broadcasted_iota(jnp.int32, (cap, sd), 1).astype(F32)
    for o in range(n_sn):
        hit = jnp.where(column(rowv, o) == lane_rows, 1.0, 0.0).astype(BF16)
        one[o * cap : (o + 1) * cap, :sd] = hit
    put[...] = jnp.transpose(one[: n_sn * cap, :sd])

    loads[4].wait()
    for i in range(8):
        cols = pl.ds(LANES * i, LANES)
        if i > 0:
            big[: INPUTS * i, cols] = jnp.zeros((INPUTS * i, LANES), BF16)
        big[INPUTS * i : INPUTS * i + span, cols] = sk[...]
        big[INPUTS * i + span :, cols] = jnp.zeros((LANES - INPUTS * i, LANES), BF16)

    @pl.when(t >= n_tm - 2)
    def _():
        hx[12:16] = jnp.zeros((4, sd, LANES), BF16)
        ht[12 * LANES :, :] = jnp.zeros((4 * LANES, sd), BF16)

    @pl.when(t == n_tm - 1)
    def _():
        hx[8:12] = jnp.zeros((4, sd, LANES), BF16)
        ht[8 * LANES : 12 * LANES, :] = jnp.zeros((4 * LANES, sd), BF16)

    acc2[...] = jnp.zeros_like(acc2)

    def h_copy(src, dst, sem, to):
        return pltpu.make_async_remote_copy(
            src_ref=hx.at[src],
            dst_ref=hx.at[dst],
            send_sem=h_send.at[sem],
            recv_sem=h_recv.at[sem],
            device_id=(to, s),
            device_id_type=MESH,
        )

    before, after = jnp.maximum(t - 1, 0), jnp.minimum(t + 1, n_tm - 1)

    def down(q):
        return h_copy(4 + q, 8 + q, q, before)

    def onward(q):
        return h_copy(8 + q, 12 + q, 4 + q, before)

    def up(q):
        return h_copy(4 + q, q, 8 + q, after)

    def turn(c):
        ht[LANES * c : LANES * (c + 1), :] = jnp.transpose(hx[c])

    def place(q):
        def body(d, _):
            a_arrival(q, lax.rem(s + d, n_sn)).wait_recv()
            return 0

        lax.fori_loop(1, n_sn, body, 0)
        hx[4 + q] = dot(put[...], arr[q]).astype(BF16)

        @pl.when(t > 0)
        def _():
            down(q).start()

        if q >= FIRST:
            @pl.when(t < n_tm - 1)
            def _():
                up(q).start()

        turn(4 + q)

    def relay(q):
        @pl.when(t < n_tm - 1)
        def _():
            down(q).wait_recv()

            @pl.when(t > 0)
            def _():
                onward(q).start()

            turn(8 + q)

    def below(q):
        up(q).wait_recv()
        turn(q)

    def above(q):
        @pl.when(t < n_tm - 2)
        def _():
            onward(q).wait_recv()
            if 12 + q < 16 - AHEAD:
                turn(12 + q)

    def weigh(g, chunks, v):
        lhs = jnp.concatenate([hx[c] for c in chunks], axis=1)
        cols = slice(256 * v, 256 * v + 256)
        rhs = jnp.concatenate([big[LANES * (c - g) : LANES * (c - g + 1), cols] for c in chunks], axis=0)
        return dot(lhs, rhs)

    def part(g, chunks, first=False):
        for v in range(4):
            r = weigh(g, chunks, v)
            for i in range(2):
                piece = r[:, LANES * i : LANES * (i + 1)]
                hb[g, 2 * v + i] = piece if first else hb[g, 2 * v + i] + piece

    def last_part(g, chunks, rounded, kept):
        for v in range(4):
            r = weigh(g, chunks, v) + jnp.concatenate([hb[g, 2 * v], hb[g, 2 * v + 1]], axis=1)
            if kept:
                hb[g, 2 * v] = r[:, :LANES]
                hb[g, 2 * v + 1] = r[:, LANES:]
            if rounded:
                rb[v * sd : (v + 1) * sd, :] = r.astype(BF16)

    def out_copy(u):
        return pltpu.make_async_copy(hb.at[4 + u], hank.at[pl.ds(8 * u, 8)], out_sem.at[u])

    def image(g, low, high):
        lhs = jnp.concatenate(
            [ht[LANES * g + 32 * v + low : LANES * g + 32 * v + high, :] for v in range(4)], axis=1
        )
        acc2[low:high, :] = acc2[low:high, :] + dot(lhs, rb[...])

    full = span + INPUTS
    shared = list(range(4, 8 - AHEAD))
    ahead = list(range(FIRST, 4))
    later = list(range(8 - AHEAD, 8))

    place(0)
    place(1)
    for g in ahead + shared:
        part(g, [4, 5], True)
    relay(0)
    place(2)
    relay(1)
    for g in ahead + shared:
        part(g, [8, 9])

    @pl.when(t > 0)
    def _():
        below(1)

    place(3)
    for g in ahead + shared:
        part(g, [6, 7])
    relay(2)

    @pl.when(t == n_tm - 1)
    def _():
        for g in later:
            for v in range(4):
                rb[v * sd : (v + 1) * sd, :] = weigh(g, list(range(g, 8)), v).astype(BF16)
            image(g, 0, full)

    above(0)
    part(4, [10, 12])

    @pl.when(t > 0)
    def _():
        below(2)
        part(1, [1, 2])
        part(2, [2, 10])
        below(3)
        last_part(1, [3], True, False)
        image(1, 0, full)

    relay(3)

    @pl.when(t > 0)
    def _():
        last_part(2, [3], True, False)
        image(2, 0, full)
        part(3, [10])
        last_part(3, [3, 11], True, False)
        image(3, 0, full)

    half_span = span // n_xl

    def s0_copy(a):
        return pltpu.make_async_remote_copy(
            src_ref=tot.at[a, pl.ds((1 - k) * zh, zh)],
            dst_ref=s0b.at[a],
            send_sem=s0_send.at[a],
            recv_sem=s0_recv.at[a],
            device_id=(t, s + 1 - 2 * k),
            device_id_type=MESH,
        )

    for g in shared:
        last_part(g, [11], True, True)
        out_copy(g - 4).start()
        if g < shared[-1]:
            image(g, 0, full)
            continue
        for a in range(n_xl):
            low = half_span * a
            image(g, low + INPUTS if a else 0, low + half_span + INPUTS)
            whole = acc2[low : low + half_span, :LANES]
            whole = whole + acc2[low + INPUTS : low + half_span + INPUTS, LANES:]
            tot[a] = whole.reshape(tot.shape[1:])
            s0_copy(a).start()

    def part_later(rel, first):
        lhs = jnp.concatenate(
            [jnp.concatenate([hx[g + c] for c in rel], axis=1) for g in later], axis=0
        )
        for v in range(4):
            r = dot(lhs, big[LANES * rel[0] : LANES * (rel[-1] + 1), 256 * v : 256 * v + 256])
            for n, g in enumerate(later):
                for i in range(2):
                    piece = r[sd * n : sd * (n + 1), LANES * i : LANES * (i + 1)]
                    hb[g, 2 * v + i] = piece if first else hb[g, 2 * v + i] + piece

    part_later([0, 1], True)

    me = xl * n_xy + xy

    def s1_copy(a, b):
        return pltpu.make_async_remote_copy(
            src_ref=mid.at[a, b],
            dst_ref=s1b.at[me],
            send_sem=s1_send.at[a, b],
            recv_sem=s1_recv.at[me],
            device_id=(a * n_z + z, b * 2 + k),
            device_id_type=MESH,
        )

    def s1_arrival(e):
        return pltpu.make_async_remote_copy(
            src_ref=mid.at[0, 0],
            dst_ref=s1b.at[e],
            send_sem=s1_send.at[0, 0],
            recv_sem=s1_recv.at[e],
            device_id=(t, s),
            device_id_type=MESH,
        )

    for a in range(n_xl):
        s0_copy(a).wait_recv()
        for c in range(zh):
            mid[a, :, c] = tot[a, k * zh + c] + s0b[a, c]

        for d in sorted(range(n_xy), key=lambda d: -min(d % 4, 4 - d % 4)):
            b = lax.rem(xy + d, n_xy)
            if d:
                s1_copy(a, b).start()
            else:
                @pl.when(a != xl)
                def _():
                    s1_copy(a, b).start()


    s1b[me] = mid[xl, xy]
    part_later([2, 3], False)

    def s1_wait(d, _):
        s1_arrival(lax.rem(me + d, n_xl * n_xy)).wait_recv()
        return 0

    lax.fori_loop(1, n_xl * n_xy, s1_wait, 0)
    m2[...] = jnp.sum(s1b[...], axis=0)

    def s2_copy(c, kk):
        return pltpu.make_async_remote_copy(
            src_ref=m2.at[c],
            dst_ref=s2b.at[z],
            send_sem=s2_send.at[c, kk],
            recv_sem=s2_recv.at[z],
            device_id=(xl * n_z + k * zh + c, s - k + kk),
            device_id_type=MESH,
        )

    def s2_arrival(e):
        return pltpu.make_async_remote_copy(
            src_ref=m2.at[0],
            dst_ref=s2b.at[e],
            send_sem=s2_send.at[0, 0],
            recv_sem=s2_recv.at[e],
            device_id=(t, s),
            device_id_type=MESH,
        )

    for c in range(zh):
        for kk in range(2):
            @pl.when((k * zh + c != z) | (k != kk))
            def _():
                s2_copy(c, kk).start()

    @pl.when(z // zh == k)
    def _():
        s2b[z] = m2[z - k * zh]

    for g in later:
        above(g - 4)
    part_later([4, 5, 6, 7, 8], False)
    for g in later:
        out_copy(g - 4).start()

    for e in range(n_z):
        @pl.when((e != z) | (z // zh != k))
        def _():
            s2_arrival(e).wait_recv()

    done = jnp.sum(s2b[...], axis=0)
    half = tot.shape[3] // 2
    col[...] = jnp.where(k == 0, done[:half], done[half:]) * scale

    for u in range(4):
        out_copy(u).wait()
    for q in range(4):
        def body(d, _):
            a_copy(q, d).wait_send()
            return 0

        lax.fori_loop(1, n_sn, body, 0)

    @pl.when(t > 0)
    def _():
        for q in range(4):
            down(q).wait_send()

    @pl.when(t < n_tm - 1)
    def _():
        for q in range(FIRST, 4):
            up(q).wait_send()

        @pl.when(t > 0)
        def _():
            for q in range(4):
                onward(q).wait_send()

    for a in range(n_xl):
        s0_copy(a).wait_send()

        def body(b, _):
            @pl.when((a != xl) | (b != xy))
            def _():
                s1_copy(a, b).wait_send()

            return 0

        lax.fori_loop(0, n_xy, body, 0)
    for c in range(zh):
        for kk in range(2):
            @pl.when((k * zh + c != z) | (k != kk))
            def _():
                s2_copy(c, kk).wait_send()


def flush(hank, col, hank_out, col_out, sems):
    copies = [pltpu.make_async_copy(col, col_out, sems.at[0])]
    for u in range(16):
        part = pl.ds(2 * u, 2)
        copies.append(pltpu.make_async_copy(hank.at[part], hank_out.at[part], sems.at[1 + u]))
    for c in copies:
        c.start()
    for c in copies:
        c.wait()


def solution(mesh):
    n_tm, n_sn = mesh.shape["tm"], mesh.shape["sensor"]
    n_xl = 2
    n_z = n_tm // n_xl
    n_xy = n_sn // 2

    def local(state, sketch, cell, row):
        cells, width = state.shape
        span, cols = sketch.shape
        cap = cell.shape[2]
        sd = n_sn * cap // 2
        steps = width // INPUTS
        slots = n_sn * cap
        own_rows = span // (n_tm * n_sn)
        tr = 2 * own_rows
        zh = n_z // 2
        scale = 1.0 / math.sqrt(sd * n_sn * steps * n_tm)
        hbm = pl.BlockSpec(memory_space=pl.ANY)
        dma = pltpu.SemaphoreType.DMA
        hank, col = pl.pallas_call(
            functools.partial(kernel, n_tm, n_sn, n_xl, 1, scale),
            out_shape=(
                jax.ShapeDtypeStruct((steps, sd, cols), F32),
                jax.ShapeDtypeStruct((own_rows, cols), F32),
            ),
            in_specs=[hbm] * 4,
            out_specs=(hbm, pl.BlockSpec(memory_space=pltpu.VMEM)),
            scratch_shapes=[
                pltpu.VMEM((cells, width), BF16),
                pltpu.VMEM((span, cols), BF16),
                pltpu.VMEM(cell.shape, jnp.int32),
                pltpu.VMEM(row.shape, jnp.int32),
                pltpu.VMEM((slots, cells), BF16),
                pltpu.VMEM((sd, slots), BF16),
                pltpu.VMEM((4, slots, LANES), BF16),
                pltpu.VMEM((4, slots, LANES), BF16),
                pltpu.VMEM((16, sd, LANES), BF16),
                pltpu.VMEM((16 * LANES, sd), BF16),
                pltpu.VMEM((span + LANES, 8 * LANES), BF16),
                pltpu.VMEM((8, 8, sd, LANES), F32),
                pltpu.VMEM((4 * sd, 2 * LANES), BF16),
                pltpu.VMEM((span + INPUTS, 2 * LANES), F32),
                pltpu.VMEM((n_xl, n_z, n_xy, tr, LANES), F32),
                pltpu.VMEM((n_xl, zh, n_xy, tr, LANES), F32),
                pltpu.VMEM((n_xl, n_xy, zh, tr, LANES), F32),
                pltpu.VMEM((n_xl * n_xy, zh, tr, LANES), F32),
                pltpu.VMEM((zh, tr, LANES), F32),
                pltpu.VMEM((n_z, tr, LANES), F32),
                dma((5,)),
                dma((4, n_sn)),
                dma((4, n_sn)),
                dma((12,)),
                dma((12,)),
                dma((4,)),
                dma((n_xl,)),
                dma((n_xl,)),
                dma((n_xl, n_xy)),
                dma((n_xl * n_xy,)),
                dma((zh, 2)),
                dma((n_z,)),
            ],
            compiler_params=pltpu.CompilerParams(
                collective_id=0, has_side_effects=True, vmem_limit_bytes=40 * 2**20
            ),
        )(*[pltpu.with_memory_space_constraint(v, pltpu.HBM) for v in (state, sketch, cell, row)])
        return pl.pallas_call(
            flush,
            out_shape=(
                jax.ShapeDtypeStruct(hank.shape, F32),
                jax.ShapeDtypeStruct(col.shape, F32),
            ),
            in_specs=[hbm] * 2,
            out_specs=(hbm, hbm),
            scratch_shapes=[dma((17,))],
            compiler_params=pltpu.CompilerParams(vmem_limit_bytes=2**20),
        )(hank, col)

    placed = (P("sensor", "tm"), P(), P("sensor", None, None), P("sensor", None, None))
    return jax.shard_map(
        local,
        mesh=mesh,
        in_specs=placed,
        out_specs=(P("tm", "sensor", None), P(("tm", "sensor"), None)),
        check_vma=False,
    )
```

```python
import functools
import math

import jax
import jax.numpy as jnp
from jax import lax
from jax.experimental import pallas as pl
from jax.experimental.pallas import tpu as pltpu
from jax.sharding import PartitionSpec as P

INPUTS = 16
KC = 64
LANES = 128
MESH = pl.DeviceIdType.MESH
AHEAD = 3
FIRST = 4 - AHEAD
F32 = jnp.float32
BF16 = jnp.bfloat16


def dot(a, b):
    return jnp.dot(a, b, preferred_element_type=F32)


def kernel(
    n_tm, n_sn, n_xl, n_xh, scale,
    state, sketch, cell, row, hank, col,
    st, sk, cellv, rowv, one, put, sendb, arr, hx, ht, big, hb, rb, acc2, tot, s0b, mid, s1b, m2, s2b,
    ld_sem, a_send, a_recv, h_send, h_recv, out_sem, s0_send, s0_recv, s1_send, s1_recv, s2_send, s2_recv,
):
    t = lax.axis_index("tm")
    s = lax.axis_index("sensor")
    n_z = n_tm // n_xl
    n_xy = n_sn // 2
    zh = n_z // 2
    xl = t // n_z
    z = lax.rem(t, n_z)
    xy = s // 2
    k = lax.rem(s, 2)
    cap = cellv.shape[2]
    sd = hx.shape[1]
    span = sk.shape[0]
    cells = st.shape[0]

    loads = [
        pltpu.make_async_copy(cell, cellv, ld_sem.at[0]),
        pltpu.make_async_copy(row, rowv, ld_sem.at[1]),
        pltpu.make_async_copy(state.at[:, pl.ds(0, 256)], st.at[:, pl.ds(0, 256)], ld_sem.at[2]),
        pltpu.make_async_copy(state.at[:, pl.ds(256, 256)], st.at[:, pl.ds(256, 256)], ld_sem.at[3]),
        pltpu.make_async_copy(sketch, sk, ld_sem.at[4]),
    ]
    for c in loads:
        c.start()

    barrier = pltpu.get_barrier_semaphore()

    def greet(tt, ss):
        pl.semaphore_signal(barrier, inc=1, device_id=(tt, ss), device_id_type=MESH)

    def greet_line(d, _):
        greet(xl * n_z + lax.rem(z + d, n_z), 2 * xy + z // zh)
        return 0

    def greet_sensor(d, _):
        greet(t, lax.rem(s + d, n_sn))
        return 0

    def greet_plane(b, _):
        greet(lax.rem(t + n_z, n_tm), 2 * b + k)
        return 0

    lax.fori_loop(1, n_sn, greet_sensor, 0)
    lax.fori_loop(1, n_z, greet_line, 0)
    lax.fori_loop(0, n_xy, greet_plane, 0)

    @pl.when(t < n_tm - 1)
    def _():
        greet(t + 1, s)

    @pl.when(t > 0)
    def _():
        greet(t - 1, s)

    n_greet = n_sn - 1 + n_xy + 2 * zh - jnp.where(z // zh == k, 2, 0)
    n_greet = n_greet + jnp.where(t > 0, 1, 0) + jnp.where(t < n_tm - 1, 1, 0)

    loads[0].wait()
    eye = lax.broadcasted_iota(jnp.int32, (cap, cap), 0) == lax.broadcasted_iota(jnp.int32, (cap, cap), 1)

    def column(ref, o):
        line = ref[0, o : o + 1, :].astype(F32)
        return jnp.sum(jnp.where(eye, jnp.broadcast_to(line, (cap, cap)), 0.0), axis=1, keepdims=True)

    lane_cells = lax.broadcasted_iota(jnp.int32, (cap, cells), 1).astype(F32)
    for o in range(n_sn):
        one[o * cap : (o + 1) * cap, :] = jnp.where(column(cellv, o) == lane_cells, 1.0, 0.0).astype(BF16)

    def pick(half):
        res = dot(one[...], st[:, 256 * half : 256 * half + 256]).astype(BF16)
        sendb[2 * half] = res[:, :LANES]
        sendb[2 * half + 1] = res[:, LANES:]

    def a_copy(q, d):
        dst = lax.rem(s + d, n_sn)
        return pltpu.make_async_remote_copy(
            src_ref=sendb.at[q, pl.ds(pl.multiple_of(dst * cap, cap), cap)],
            dst_ref=arr.at[q, pl.ds(pl.multiple_of(s * cap, cap), cap)],
            send_sem=a_send.at[q, d],
            recv_sem=a_recv.at[q, s],
            device_id=(t, dst),
            device_id_type=MESH,
        )

    def a_arrival(q, src):
        return pltpu.make_async_remote_copy(
            src_ref=sendb.at[q, pl.ds(pl.multiple_of(src * cap, cap), cap)],
            dst_ref=arr.at[q, pl.ds(pl.multiple_of(src * cap, cap), cap)],
            send_sem=a_send.at[q, 0],
            recv_sem=a_recv.at[q, src],
            device_id=(t, src),
            device_id_type=MESH,
        )

    def exchange(q):
        for d in sorted(range(1, n_sn), key=lambda d: (-min(d // 2 % 4, 4 - d // 2 % 4), d)):
            a_copy(q, d).start()
        own = pl.ds(pl.multiple_of(s * cap, cap), cap)
        arr[q, own] = sendb[q, own]

    loads[2].wait()
    pick(0)
    pl.semaphore_wait(barrier, n_greet)
    exchange(0)
    exchange(1)
    loads[3].wait()
    pick(1)
    exchange(2)
    exchange(3)

    loads[1].wait()
    lane_rows = lax.broadcasted_iota(jnp.int32, (cap, sd), 1).astype(F32)
    for o in range(n_sn):
        hit = jnp.where(column(rowv, o) == lane_rows, 1.0, 0.0).astype(BF16)
        one[o * cap : (o + 1) * cap, :sd] = hit
    put[...] = jnp.transpose(one[: n_sn * cap, :sd])

    loads[4].wait()
    for i in range(8):
        cols = pl.ds(LANES * i, LANES)
        if i > 0:
            big[: INPUTS * i, cols] = jnp.zeros((INPUTS * i, LANES), BF16)
        big[INPUTS * i : INPUTS * i + span, cols] = sk[...]
        big[INPUTS * i + span :, cols] = jnp.zeros((LANES - INPUTS * i, LANES), BF16)

    @pl.when(t >= n_tm - 2)
    def _():
        hx[12:16] = jnp.zeros((4, sd, LANES), BF16)
        ht[12 * LANES :, :] = jnp.zeros((4 * LANES, sd), BF16)

    @pl.when(t == n_tm - 1)
    def _():
        hx[8:12] = jnp.zeros((4, sd, LANES), BF16)
        ht[8 * LANES : 12 * LANES, :] = jnp.zeros((4 * LANES, sd), BF16)

    acc2[...] = jnp.zeros_like(acc2)

    def h_copy(src, dst, sem, to):
        return pltpu.make_async_remote_copy(
            src_ref=hx.at[src],
            dst_ref=hx.at[dst],
            send_sem=h_send.at[sem],
            recv_sem=h_recv.at[sem],
            device_id=(to, s),
            device_id_type=MESH,
        )

    before, after = jnp.maximum(t - 1, 0), jnp.minimum(t + 1, n_tm - 1)

    def down(q):
        return h_copy(4 + q, 8 + q, q, before)

    def onward(q):
        return h_copy(8 + q, 12 + q, 4 + q, before)

    def up(q):
        return h_copy(4 + q, q, 8 + q, after)

    def turn(c):
        ht[LANES * c : LANES * (c + 1), :] = jnp.transpose(hx[c])

    def place(q):
        def body(d, _):
            a_arrival(q, lax.rem(s + d, n_sn)).wait_recv()
            return 0

        lax.fori_loop(1, n_sn, body, 0)
        hx[4 + q] = dot(put[...], arr[q]).astype(BF16)

        @pl.when(t > 0)
        def _():
            down(q).start()

        if q >= FIRST:
            @pl.when(t < n_tm - 1)
            def _():
                up(q).start()

        turn(4 + q)

    def relay(q):
        @pl.when(t < n_tm - 1)
        def _():
            down(q).wait_recv()

            @pl.when(t > 0)
            def _():
                onward(q).start()

            turn(8 + q)

    def below(q):
        up(q).wait_recv()
        turn(q)

    def above(q):
        @pl.when(t < n_tm - 2)
        def _():
            onward(q).wait_recv()
            if 12 + q < 16 - AHEAD:
                turn(12 + q)

    def weigh(g, chunks, v):
        lhs = jnp.concatenate([hx[c] for c in chunks], axis=1)
        cols = slice(256 * v, 256 * v + 256)
        rhs = jnp.concatenate([big[LANES * (c - g) : LANES * (c - g + 1), cols] for c in chunks], axis=0)
        return dot(lhs, rhs)

    def part(g, chunks, first=False):
        for v in range(4):
            r = weigh(g, chunks, v)
            for i in range(2):
                piece = r[:, LANES * i : LANES * (i + 1)]
                hb[g, 2 * v + i] = piece if first else hb[g, 2 * v + i] + piece

    def last_part(g, chunks, rounded, kept):
        for v in range(4):
            r = weigh(g, chunks, v) + jnp.concatenate([hb[g, 2 * v], hb[g, 2 * v + 1]], axis=1)
            if kept:
                hb[g, 2 * v] = r[:, :LANES]
                hb[g, 2 * v + 1] = r[:, LANES:]
            if rounded:
                rb[v * sd : (v + 1) * sd, :] = r.astype(BF16)

    def out_copy(u, v):
        return pltpu.make_async_copy(
            hb.at[4 + u, pl.ds(2 * v, 2)], hank.at[pl.ds(8 * u + 2 * v, 2)], out_sem.at[u, v]
        )

    def image(g, low, high):
        lhs = jnp.concatenate(
            [ht[LANES * g + 32 * v + low : LANES * g + 32 * v + high, :] for v in range(4)], axis=1
        )
        acc2[low:high, :] = acc2[low:high, :] + dot(lhs, rb[...])

    full = span + INPUTS
    shared = list(range(4, 8 - AHEAD))
    ahead = list(range(FIRST, 4))
    later = list(range(8 - AHEAD, 8))

    place(0)
    place(1)
    for g in ahead + shared:
        part(g, [4, 5], True)
    place(2)
    place(3)
    relay(0)
    for g in ahead:
        part(g, [6, 7])
    relay(1)
    for g in shared:
        part(g, [6, 7])

    @pl.when(t == n_tm - 1)
    def _():
        for g in later:
            for v in range(4):
                rb[v * sd : (v + 1) * sd, :] = weigh(g, list(range(g, 8)), v).astype(BF16)
            image(g, 0, full)

    for g in ahead + shared:
        part(g, [8, 9])
    relay(2)

    @pl.when(t > 0)
    def _():
        below(1)
        below(2)
        part(1, [1, 2])
        part(2, [2, 10])
        below(3)
        last_part(1, [3], True, False)
        image(1, 0, full)

    relay(3)

    @pl.when(t > 0)
    def _():
        last_part(2, [3], True, False)
        image(2, 0, full)
        part(3, [10])
        last_part(3, [3, 11], True, False)
        image(3, 0, full)

    part(4, [10, 11])
    above(0)

    half_span = span // n_xl

    def s0_copy(a):
        return pltpu.make_async_remote_copy(
            src_ref=tot.at[a, pl.ds((1 - k) * zh, zh)],
            dst_ref=s0b.at[a],
            send_sem=s0_send.at[a],
            recv_sem=s0_recv.at[a],
            device_id=(t, s + 1 - 2 * k),
            device_id_type=MESH,
        )

    for g in shared:
        last_part(g, [12], True, True)
        for v in range(4):
            out_copy(g - 4, v).start()
        if g < shared[-1]:
            image(g, 0, full)
            continue
        for a in range(n_xl):
            low = half_span * a
            image(g, low + INPUTS if a else 0, low + half_span + INPUTS)
            whole = acc2[low : low + half_span, :LANES]
            whole = whole + acc2[low + INPUTS : low + half_span + INPUTS, LANES:]
            tot[a] = whole.reshape(tot.shape[1:])
            s0_copy(a).start()

    def part_later(rel, first):
        lhs = jnp.concatenate(
            [jnp.concatenate([hx[g + c] for c in rel], axis=1) for g in later], axis=0
        )
        for v in range(4):
            r = dot(lhs, big[LANES * rel[0] : LANES * (rel[-1] + 1), 256 * v : 256 * v + 256])
            for n, g in enumerate(later):
                for i in range(2):
                    piece = r[sd * n : sd * (n + 1), LANES * i : LANES * (i + 1)]
                    hb[g, 2 * v + i] = piece if first else hb[g, 2 * v + i] + piece
                if rel[-1] == 8:
                    out_copy(g - 4, v).start()

    part_later([0, 1], True)

    me = xl * n_xy + xy

    def s1_copy(a, b):
        return pltpu.make_async_remote_copy(
            src_ref=mid.at[a, b],
            dst_ref=s1b.at[me],
            send_sem=s1_send.at[a, b],
            recv_sem=s1_recv.at[me],
            device_id=(a * n_z + z, b * 2 + k),
            device_id_type=MESH,
        )

    def s1_arrival(e):
        return pltpu.make_async_remote_copy(
            src_ref=mid.at[0, 0],
            dst_ref=s1b.at[e],
            send_sem=s1_send.at[0, 0],
            recv_sem=s1_recv.at[e],
            device_id=(t, s),
            device_id_type=MESH,
        )

    for a in range(n_xl):
        s0_copy(a).wait_recv()
        for c in range(zh):
            mid[a, :, c] = tot[a, k * zh + c] + s0b[a, c]

        for d in sorted(range(n_xy), key=lambda d: -min(d % 4, 4 - d % 4)):
            b = lax.rem(xy + d, n_xy)
            if d:
                s1_copy(a, b).start()
            else:
                @pl.when(a != xl)
                def _():
                    s1_copy(a, b).start()


    s1b[me] = mid[xl, xy]
    part_later([2, 3, 4, 5], False)

    def s1_wait(d, _):
        s1_arrival(lax.rem(me + d, n_xl * n_xy)).wait_recv()
        return 0

    lax.fori_loop(1, n_xl * n_xy, s1_wait, 0)
    m2[...] = jnp.sum(s1b[...], axis=0)

    def s2_copy(c, kk):
        return pltpu.make_async_remote_copy(
            src_ref=m2.at[c],
            dst_ref=s2b.at[z],
            send_sem=s2_send.at[c, kk],
            recv_sem=s2_recv.at[z],
            device_id=(xl * n_z + k * zh + c, s - k + kk),
            device_id_type=MESH,
        )

    def s2_arrival(e):
        return pltpu.make_async_remote_copy(
            src_ref=m2.at[0],
            dst_ref=s2b.at[e],
            send_sem=s2_send.at[0, 0],
            recv_sem=s2_recv.at[e],
            device_id=(t, s),
            device_id_type=MESH,
        )

    for c in range(zh):
        for kk in range(2):
            @pl.when((k * zh + c != z) | (k != kk))
            def _():
                s2_copy(c, kk).start()

    @pl.when(z // zh == k)
    def _():
        s2b[z] = m2[z - k * zh]

    for g in later:
        above(g - 4)
    part_later([6, 7, 8], False)

    for e in range(n_z):
        @pl.when((e != z) | (z // zh != k))
        def _():
            s2_arrival(e).wait_recv()

    done = jnp.sum(s2b[...], axis=0)
    half = tot.shape[3] // 2
    col[...] = jnp.where(k == 0, done[:half], done[half:]) * scale

    for u in range(4):
        for v in range(4):
            out_copy(u, v).wait()
    for q in range(4):
        def body(d, _):
            a_copy(q, d).wait_send()
            return 0

        lax.fori_loop(1, n_sn, body, 0)

    @pl.when(t > 0)
    def _():
        for q in range(4):
            down(q).wait_send()

    @pl.when(t < n_tm - 1)
    def _():
        for q in range(FIRST, 4):
            up(q).wait_send()

        @pl.when(t > 0)
        def _():
            for q in range(4):
                onward(q).wait_send()

    for a in range(n_xl):
        s0_copy(a).wait_send()

        def body(b, _):
            @pl.when((a != xl) | (b != xy))
            def _():
                s1_copy(a, b).wait_send()

            return 0

        lax.fori_loop(0, n_xy, body, 0)
    for c in range(zh):
        for kk in range(2):
            @pl.when((k * zh + c != z) | (k != kk))
            def _():
                s2_copy(c, kk).wait_send()


def flush(hank, col, hank_out, col_out, sems):
    copies = [pltpu.make_async_copy(col, col_out, sems.at[0])]
    for u in range(16):
        part = pl.ds(2 * u, 2)
        copies.append(pltpu.make_async_copy(hank.at[part], hank_out.at[part], sems.at[1 + u]))
    for c in copies:
        c.start()
    for c in copies:
        c.wait()


def solution(mesh):
    n_tm, n_sn = mesh.shape["tm"], mesh.shape["sensor"]
    n_xl = 2
    n_z = n_tm // n_xl
    n_xy = n_sn // 2

    def local(state, sketch, cell, row):
        cells, width = state.shape
        span, cols = sketch.shape
        cap = cell.shape[2]
        sd = n_sn * cap // 2
        steps = width // INPUTS
        slots = n_sn * cap
        own_rows = span // (n_tm * n_sn)
        tr = 2 * own_rows
        zh = n_z // 2
        scale = 1.0 / math.sqrt(sd * n_sn * steps * n_tm)
        hbm = pl.BlockSpec(memory_space=pl.ANY)
        dma = pltpu.SemaphoreType.DMA
        hank, col = pl.pallas_call(
            functools.partial(kernel, n_tm, n_sn, n_xl, 1, scale),
            out_shape=(
                jax.ShapeDtypeStruct((steps, sd, cols), F32),
                jax.ShapeDtypeStruct((own_rows, cols), F32),
            ),
            in_specs=[hbm] * 4,
            out_specs=(hbm, pl.BlockSpec(memory_space=pltpu.VMEM)),
            scratch_shapes=[
                pltpu.VMEM((cells, width), BF16),
                pltpu.VMEM((span, cols), BF16),
                pltpu.VMEM(cell.shape, jnp.int32),
                pltpu.VMEM(row.shape, jnp.int32),
                pltpu.VMEM((slots, cells), BF16),
                pltpu.VMEM((sd, slots), BF16),
                pltpu.VMEM((4, slots, LANES), BF16),
                pltpu.VMEM((4, slots, LANES), BF16),
                pltpu.VMEM((16, sd, LANES), BF16),
                pltpu.VMEM((16 * LANES, sd), BF16),
                pltpu.VMEM((span + LANES, 8 * LANES), BF16),
                pltpu.VMEM((8, 8, sd, LANES), F32),
                pltpu.VMEM((4 * sd, 2 * LANES), BF16),
                pltpu.VMEM((span + INPUTS, 2 * LANES), F32),
                pltpu.VMEM((n_xl, n_z, n_xy, tr, LANES), F32),
                pltpu.VMEM((n_xl, zh, n_xy, tr, LANES), F32),
                pltpu.VMEM((n_xl, n_xy, zh, tr, LANES), F32),
                pltpu.VMEM((n_xl * n_xy, zh, tr, LANES), F32),
                pltpu.VMEM((zh, tr, LANES), F32),
                pltpu.VMEM((n_z, tr, LANES), F32),
                dma((5,)),
                dma((4, n_sn)),
                dma((4, n_sn)),
                dma((12,)),
                dma((12,)),
                dma((4, 4)),
                dma((n_xl,)),
                dma((n_xl,)),
                dma((n_xl, n_xy)),
                dma((n_xl * n_xy,)),
                dma((zh, 2)),
                dma((n_z,)),
            ],
            compiler_params=pltpu.CompilerParams(
                collective_id=0, has_side_effects=True, vmem_limit_bytes=40 * 2**20
            ),
        )(*[pltpu.with_memory_space_constraint(v, pltpu.HBM) for v in (state, sketch, cell, row)])
        return pl.pallas_call(
            flush,
            out_shape=(
                jax.ShapeDtypeStruct(hank.shape, F32),
                jax.ShapeDtypeStruct(col.shape, F32),
            ),
            in_specs=[hbm] * 2,
            out_specs=(hbm, hbm),
            scratch_shapes=[dma((17,))],
            compiler_params=pltpu.CompilerParams(vmem_limit_bytes=2**20),
        )(hank, col)

    placed = (P("sensor", "tm"), P(), P("sensor", None, None), P("sensor", None, None))
    return jax.shard_map(
        local,
        mesh=mesh,
        in_specs=placed,
        out_specs=(P("tm", "sensor", None), P(("tm", "sensor"), None)),
        check_vma=False,
    )
```

```python
import functools
import math

import jax
import jax.numpy as jnp
from jax import lax
from jax.experimental import pallas as pl
from jax.experimental.pallas import tpu as pltpu
from jax.sharding import PartitionSpec as P

INPUTS = 16
KC = 64
LANES = 128
MESH = pl.DeviceIdType.MESH
AHEAD = 3
FIRST = 4 - AHEAD
F32 = jnp.float32
BF16 = jnp.bfloat16


def dot(a, b):
    return jnp.dot(a, b, preferred_element_type=F32)


def kernel(
    n_tm, n_sn, n_xl, n_xh, scale,
    state, sketch, cell, row, hank, col,
    st, sk, cellv, rowv, one, put, sendb, arr, hx, ht, big, hb, rb, acc2, tot, s0b, mid, s1b, m2, s2b, via,
    ld_sem, a_send, a_recv, h_send, h_recv, out_sem, s0_send, s0_recv, s1_send, s1_recv, s2_send, s2_recv, via_send, via_recv,
):
    t = lax.axis_index("tm")
    s = lax.axis_index("sensor")
    n_z = n_tm // n_xl
    n_xy = n_sn // 2
    zh = n_z // 2
    xl = t // n_z
    z = lax.rem(t, n_z)
    xy = s // 2
    k = lax.rem(s, 2)
    cap = cellv.shape[2]
    sd = hx.shape[1]
    span = sk.shape[0]
    cells = st.shape[0]

    loads = [
        pltpu.make_async_copy(cell, cellv, ld_sem.at[0]),
        pltpu.make_async_copy(row, rowv, ld_sem.at[1]),
        pltpu.make_async_copy(state.at[:, pl.ds(0, 256)], st.at[:, pl.ds(0, 256)], ld_sem.at[2]),
        pltpu.make_async_copy(state.at[:, pl.ds(256, 256)], st.at[:, pl.ds(256, 256)], ld_sem.at[3]),
        pltpu.make_async_copy(sketch, sk, ld_sem.at[4]),
    ]
    for c in loads:
        c.start()

    barrier = pltpu.get_barrier_semaphore()

    def greet(tt, ss):
        pl.semaphore_signal(barrier, inc=1, device_id=(tt, ss), device_id_type=MESH)

    def greet_line(d, _):
        greet(xl * n_z + lax.rem(z + d, n_z), 2 * xy + z // zh)
        return 0

    def greet_sensor(d, _):
        greet(t, lax.rem(s + d, n_sn))
        return 0

    def greet_plane(b, _):
        greet(lax.rem(t + n_z, n_tm), 2 * b + k)
        return 0

    lax.fori_loop(1, n_sn, greet_sensor, 0)
    lax.fori_loop(1, n_z, greet_line, 0)
    lax.fori_loop(0, n_xy, greet_plane, 0)

    @pl.when(t < n_tm - 1)
    def _():
        greet(t + 1, s)

    @pl.when(t > 0)
    def _():
        greet(t - 1, s)

    n_greet = n_sn - 1 + n_xy + 2 * zh - jnp.where(z // zh == k, 2, 0)
    n_greet = n_greet + jnp.where(t > 0, 1, 0) + jnp.where(t < n_tm - 1, 1, 0)

    loads[0].wait()
    eye = lax.broadcasted_iota(jnp.int32, (cap, cap), 0) == lax.broadcasted_iota(jnp.int32, (cap, cap), 1)

    def column(ref, o):
        line = ref[0, o : o + 1, :].astype(F32)
        return jnp.sum(jnp.where(eye, jnp.broadcast_to(line, (cap, cap)), 0.0), axis=1, keepdims=True)

    lane_cells = lax.broadcasted_iota(jnp.int32, (cap, cells), 1).astype(F32)
    for o in range(n_sn):
        one[o * cap : (o + 1) * cap, :] = jnp.where(column(cellv, o) == lane_cells, 1.0, 0.0).astype(BF16)

    def pick(half):
        res = dot(one[...], st[:, 256 * half : 256 * half + 256]).astype(BF16)
        sendb[2 * half] = res[:, :LANES]
        sendb[2 * half + 1] = res[:, LANES:]

    def a_copy(q, d):
        dst = lax.rem(s + d, n_sn)
        return pltpu.make_async_remote_copy(
            src_ref=sendb.at[q, pl.ds(pl.multiple_of(dst * cap, cap), cap)],
            dst_ref=arr.at[q, pl.ds(pl.multiple_of(s * cap, cap), cap)],
            send_sem=a_send.at[q, d],
            recv_sem=a_recv.at[q, s],
            device_id=(t, dst),
            device_id_type=MESH,
        )

    def a_arrival(q, src):
        return pltpu.make_async_remote_copy(
            src_ref=sendb.at[q, pl.ds(pl.multiple_of(src * cap, cap), cap)],
            dst_ref=arr.at[q, pl.ds(pl.multiple_of(src * cap, cap), cap)],
            send_sem=a_send.at[q, 0],
            recv_sem=a_recv.at[q, src],
            device_id=(t, src),
            device_id_type=MESH,
        )

    detour = (4, 12) if n_sn == 16 else ()

    def along(steps):
        line = s // 8 * 4 + lax.rem(s // 2 + 4 + steps, 4)
        return 2 * line + k

    def via_copy(q, j):
        dst = lax.rem(s + detour[j], n_sn)
        return pltpu.make_async_remote_copy(
            src_ref=sendb.at[q, pl.ds(pl.multiple_of(dst * cap, cap), cap)],
            dst_ref=via.at[q, j],
            send_sem=a_send.at[q, detour[j]],
            recv_sem=via_recv.at[q, j],
            device_id=(t, along(-1)),
            device_id_type=MESH,
        )

    def pass_copy(q, j):
        origin = along(1)
        return pltpu.make_async_remote_copy(
            src_ref=via.at[q, j],
            dst_ref=arr.at[q, pl.ds(pl.multiple_of(origin * cap, cap), cap)],
            send_sem=via_send.at[q, j],
            recv_sem=a_recv.at[q, origin],
            device_id=(t, lax.rem(origin + detour[j], n_sn)),
            device_id_type=MESH,
        )

    def pass_on(q):
        for j in range(len(detour)):
            via_copy(q, j).wait_recv()
            pass_copy(q, j).start()

    def exchange(q):
        for j in range(len(detour)):
            via_copy(q, j).start()
        for d in sorted(range(1, n_sn), key=lambda d: (-min(d // 2 % 4, 4 - d // 2 % 4), d)):
            if d not in detour:
                a_copy(q, d).start()
        own = pl.ds(pl.multiple_of(s * cap, cap), cap)
        arr[q, own] = sendb[q, own]

    loads[2].wait()
    pick(0)
    pl.semaphore_wait(barrier, n_greet)
    exchange(0)
    exchange(1)
    loads[3].wait()
    pick(1)
    exchange(2)
    exchange(3)

    loads[1].wait()
    lane_rows = lax.broadcasted_iota(jnp.int32, (cap, sd), 1).astype(F32)
    for o in range(n_sn):
        hit = jnp.where(column(rowv, o) == lane_rows, 1.0, 0.0).astype(BF16)
        one[o * cap : (o + 1) * cap, :sd] = hit
    put[...] = jnp.transpose(one[: n_sn * cap, :sd])

    loads[4].wait()
    for i in range(8):
        cols = pl.ds(LANES * i, LANES)
        if i > 0:
            big[: INPUTS * i, cols] = jnp.zeros((INPUTS * i, LANES), BF16)
        big[INPUTS * i : INPUTS * i + span, cols] = sk[...]
        big[INPUTS * i + span :, cols] = jnp.zeros((LANES - INPUTS * i, LANES), BF16)

    @pl.when(t >= n_tm - 2)
    def _():
        hx[12:16] = jnp.zeros((4, sd, LANES), BF16)
        ht[12 * LANES :, :] = jnp.zeros((4 * LANES, sd), BF16)

    @pl.when(t == n_tm - 1)
    def _():
        hx[8:12] = jnp.zeros((4, sd, LANES), BF16)
        ht[8 * LANES : 12 * LANES, :] = jnp.zeros((4 * LANES, sd), BF16)

    acc2[...] = jnp.zeros_like(acc2)

    def h_copy(src, dst, sem, to):
        return pltpu.make_async_remote_copy(
            src_ref=hx.at[src],
            dst_ref=hx.at[dst],
            send_sem=h_send.at[sem],
            recv_sem=h_recv.at[sem],
            device_id=(to, s),
            device_id_type=MESH,
        )

    before, after = jnp.maximum(t - 1, 0), jnp.minimum(t + 1, n_tm - 1)

    def down(q):
        return h_copy(4 + q, 8 + q, q, before)

    def onward(q):
        return h_copy(8 + q, 12 + q, 4 + q, before)

    def up(q):
        return h_copy(4 + q, q, 8 + q, after)

    def turn(c):
        ht[LANES * c : LANES * (c + 1), :] = jnp.transpose(hx[c])

    def place(q):
        def body(d, _):
            a_arrival(q, lax.rem(s + d, n_sn)).wait_recv()
            return 0

        lax.fori_loop(1, n_sn, body, 0)
        hx[4 + q] = dot(put[...], arr[q]).astype(BF16)

        @pl.when(t > 0)
        def _():
            down(q).start()

        if q >= FIRST:
            @pl.when(t < n_tm - 1)
            def _():
                up(q).start()

        turn(4 + q)

    def relay(q):
        @pl.when(t < n_tm - 1)
        def _():
            down(q).wait_recv()

            @pl.when(t > 0)
            def _():
                onward(q).start()

            turn(8 + q)

    def below(q):
        up(q).wait_recv()
        turn(q)

    def above(q):
        @pl.when(t < n_tm - 2)
        def _():
            onward(q).wait_recv()
            if 12 + q < 16 - AHEAD:
                turn(12 + q)

    def weigh(g, chunks, v):
        lhs = jnp.concatenate([hx[c] for c in chunks], axis=1)
        cols = slice(256 * v, 256 * v + 256)
        rhs = jnp.concatenate([big[LANES * (c - g) : LANES * (c - g + 1), cols] for c in chunks], axis=0)
        return dot(lhs, rhs)

    def part(g, chunks, first=False):
        for v in range(4):
            r = weigh(g, chunks, v)
            for i in range(2):
                piece = r[:, LANES * i : LANES * (i + 1)]
                hb[g, 2 * v + i] = piece if first else hb[g, 2 * v + i] + piece

    def last_part(g, chunks, rounded, kept):
        for v in range(4):
            r = weigh(g, chunks, v) + jnp.concatenate([hb[g, 2 * v], hb[g, 2 * v + 1]], axis=1)
            if kept:
                hb[g, 2 * v] = r[:, :LANES]
                hb[g, 2 * v + 1] = r[:, LANES:]
            if rounded:
                rb[v * sd : (v + 1) * sd, :] = r.astype(BF16)

    def out_copy(u, v):
        return pltpu.make_async_copy(
            hb.at[4 + u, pl.ds(2 * v, 2)], hank.at[pl.ds(8 * u + 2 * v, 2)], out_sem.at[u, v]
        )

    def image(g, low, high):
        lhs = jnp.concatenate(
            [ht[LANES * g + 32 * v + low : LANES * g + 32 * v + high, :] for v in range(4)], axis=1
        )
        acc2[low:high, :] = acc2[low:high, :] + dot(lhs, rb[...])

    full = span + INPUTS
    shared = list(range(4, 8 - AHEAD))
    ahead = list(range(FIRST, 4))
    later = list(range(8 - AHEAD, 8))

    pass_on(0)
    pass_on(1)
    place(0)
    pass_on(2)
    place(1)
    pass_on(3)
    for g in ahead + shared:
        part(g, [4, 5], True)
    place(2)
    place(3)
    relay(0)
    for g in ahead:
        part(g, [6, 7])
    relay(1)
    for g in shared:
        part(g, [6, 7])

    @pl.when(t == n_tm - 1)
    def _():
        for g in later:
            for v in range(4):
                rb[v * sd : (v + 1) * sd, :] = weigh(g, list(range(g, 8)), v).astype(BF16)
            image(g, 0, full)

    for g in ahead + shared:
        part(g, [8, 9])
    relay(2)

    @pl.when(t > 0)
    def _():
        below(1)
        below(2)
        part(1, [1, 2])
        part(2, [2, 10])
        below(3)
        last_part(1, [3], True, False)
        image(1, 0, full)

    relay(3)

    @pl.when(t > 0)
    def _():
        last_part(2, [3], True, False)
        image(2, 0, full)
        part(3, [10])
        last_part(3, [3, 11], True, False)
        image(3, 0, full)

    part(4, [10, 11])
    above(0)

    half_span = span // n_xl

    def s0_copy(a):
        return pltpu.make_async_remote_copy(
            src_ref=tot.at[a, pl.ds((1 - k) * zh, zh)],
            dst_ref=s0b.at[a],
            send_sem=s0_send.at[a],
            recv_sem=s0_recv.at[a],
            device_id=(t, s + 1 - 2 * k),
            device_id_type=MESH,
        )

    for g in shared:
        last_part(g, [12], True, True)
        for v in range(4):
            out_copy(g - 4, v).start()
        if g < shared[-1]:
            image(g, 0, full)
            continue
        for a in range(n_xl):
            low = half_span * a
            image(g, low + INPUTS if a else 0, low + half_span + INPUTS)
            whole = acc2[low : low + half_span, :LANES]
            whole = whole + acc2[low + INPUTS : low + half_span + INPUTS, LANES:]
            tot[a] = whole.reshape(tot.shape[1:])
            s0_copy(a).start()

    def part_later(rel, first):
        lhs = jnp.concatenate(
            [jnp.concatenate([hx[g + c] for c in rel], axis=1) for g in later], axis=0
        )
        for v in range(4):
            r = dot(lhs, big[LANES * rel[0] : LANES * (rel[-1] + 1), 256 * v : 256 * v + 256])
            for n, g in enumerate(later):
                for i in range(2):
                    piece = r[sd * n : sd * (n + 1), LANES * i : LANES * (i + 1)]
                    hb[g, 2 * v + i] = piece if first else hb[g, 2 * v + i] + piece
                if rel[-1] == 8:
                    out_copy(g - 4, v).start()

    part_later([0, 1], True)

    me = xl * n_xy + xy

    def s1_copy(a, b):
        return pltpu.make_async_remote_copy(
            src_ref=mid.at[a, b],
            dst_ref=s1b.at[me],
            send_sem=s1_send.at[a, b],
            recv_sem=s1_recv.at[me],
            device_id=(a * n_z + z, b * 2 + k),
            device_id_type=MESH,
        )

    def s1_arrival(e):
        return pltpu.make_async_remote_copy(
            src_ref=mid.at[0, 0],
            dst_ref=s1b.at[e],
            send_sem=s1_send.at[0, 0],
            recv_sem=s1_recv.at[e],
            device_id=(t, s),
            device_id_type=MESH,
        )

    for a in range(n_xl):
        s0_copy(a).wait_recv()
        for c in range(zh):
            mid[a, :, c] = tot[a, k * zh + c] + s0b[a, c]

        for d in sorted(range(n_xy), key=lambda d: -min(d % 4, 4 - d % 4)):
            b = lax.rem(xy + d, n_xy)
            if d:
                s1_copy(a, b).start()
            else:
                @pl.when(a != xl)
                def _():
                    s1_copy(a, b).start()


    s1b[me] = mid[xl, xy]
    part_later([2, 3, 4, 5], False)

    def s1_wait(d, _):
        s1_arrival(lax.rem(me + d, n_xl * n_xy)).wait_recv()
        return 0

    lax.fori_loop(1, n_xl * n_xy, s1_wait, 0)
    m2[...] = jnp.sum(s1b[...], axis=0)

    def s2_copy(c, kk):
        return pltpu.make_async_remote_copy(
            src_ref=m2.at[c],
            dst_ref=s2b.at[z],
            send_sem=s2_send.at[c, kk],
            recv_sem=s2_recv.at[z],
            device_id=(xl * n_z + k * zh + c, s - k + kk),
            device_id_type=MESH,
        )

    def s2_arrival(e):
        return pltpu.make_async_remote_copy(
            src_ref=m2.at[0],
            dst_ref=s2b.at[e],
            send_sem=s2_send.at[0, 0],
            recv_sem=s2_recv.at[e],
            device_id=(t, s),
            device_id_type=MESH,
        )

    for c in range(zh):
        for kk in range(2):
            @pl.when((k * zh + c != z) | (k != kk))
            def _():
                s2_copy(c, kk).start()

    @pl.when(z // zh == k)
    def _():
        s2b[z] = m2[z - k * zh]

    for g in later:
        above(g - 4)
    part_later([6, 7, 8], False)

    for e in range(n_z):
        @pl.when((e != z) | (z // zh != k))
        def _():
            s2_arrival(e).wait_recv()

    done = jnp.sum(s2b[...], axis=0)
    half = tot.shape[3] // 2
    col[...] = jnp.where(k == 0, done[:half], done[half:]) * scale

    for u in range(4):
        for v in range(4):
            out_copy(u, v).wait()
    for q in range(4):
        for j in range(len(detour)):
            pass_copy(q, j).wait_send()
    for q in range(4):
        def body(d, _):
            a_copy(q, d).wait_send()
            return 0

        lax.fori_loop(1, n_sn, body, 0)

    @pl.when(t > 0)
    def _():
        for q in range(4):
            down(q).wait_send()

    @pl.when(t < n_tm - 1)
    def _():
        for q in range(FIRST, 4):
            up(q).wait_send()

        @pl.when(t > 0)
        def _():
            for q in range(4):
                onward(q).wait_send()

    for a in range(n_xl):
        s0_copy(a).wait_send()

        def body(b, _):
            @pl.when((a != xl) | (b != xy))
            def _():
                s1_copy(a, b).wait_send()

            return 0

        lax.fori_loop(0, n_xy, body, 0)
    for c in range(zh):
        for kk in range(2):
            @pl.when((k * zh + c != z) | (k != kk))
            def _():
                s2_copy(c, kk).wait_send()


def flush(hank, col, hank_out, col_out, sems):
    copies = [pltpu.make_async_copy(col, col_out, sems.at[0])]
    for u in range(16):
        part = pl.ds(2 * u, 2)
        copies.append(pltpu.make_async_copy(hank.at[part], hank_out.at[part], sems.at[1 + u]))
    for c in copies:
        c.start()
    for c in copies:
        c.wait()


def solution(mesh):
    n_tm, n_sn = mesh.shape["tm"], mesh.shape["sensor"]
    n_xl = 2
    n_z = n_tm // n_xl
    n_xy = n_sn // 2

    def local(state, sketch, cell, row):
        cells, width = state.shape
        span, cols = sketch.shape
        cap = cell.shape[2]
        sd = n_sn * cap // 2
        steps = width // INPUTS
        slots = n_sn * cap
        own_rows = span // (n_tm * n_sn)
        tr = 2 * own_rows
        zh = n_z // 2
        scale = 1.0 / math.sqrt(sd * n_sn * steps * n_tm)
        hbm = pl.BlockSpec(memory_space=pl.ANY)
        dma = pltpu.SemaphoreType.DMA
        hank, col = pl.pallas_call(
            functools.partial(kernel, n_tm, n_sn, n_xl, 1, scale),
            out_shape=(
                jax.ShapeDtypeStruct((steps, sd, cols), F32),
                jax.ShapeDtypeStruct((own_rows, cols), F32),
            ),
            in_specs=[hbm] * 4,
            out_specs=(hbm, pl.BlockSpec(memory_space=pltpu.VMEM)),
            scratch_shapes=[
                pltpu.VMEM((cells, width), BF16),
                pltpu.VMEM((span, cols), BF16),
                pltpu.VMEM(cell.shape, jnp.int32),
                pltpu.VMEM(row.shape, jnp.int32),
                pltpu.VMEM((slots, cells), BF16),
                pltpu.VMEM((sd, slots), BF16),
                pltpu.VMEM((4, slots, LANES), BF16),
                pltpu.VMEM((4, slots, LANES), BF16),
                pltpu.VMEM((16, sd, LANES), BF16),
                pltpu.VMEM((16 * LANES, sd), BF16),
                pltpu.VMEM((span + LANES, 8 * LANES), BF16),
                pltpu.VMEM((8, 8, sd, LANES), F32),
                pltpu.VMEM((4 * sd, 2 * LANES), BF16),
                pltpu.VMEM((span + INPUTS, 2 * LANES), F32),
                pltpu.VMEM((n_xl, n_z, n_xy, tr, LANES), F32),
                pltpu.VMEM((n_xl, zh, n_xy, tr, LANES), F32),
                pltpu.VMEM((n_xl, n_xy, zh, tr, LANES), F32),
                pltpu.VMEM((n_xl * n_xy, zh, tr, LANES), F32),
                pltpu.VMEM((zh, tr, LANES), F32),
                pltpu.VMEM((n_z, tr, LANES), F32),
                pltpu.VMEM((4, 2, cap, LANES), BF16),
                dma((5,)),
                dma((4, n_sn)),
                dma((4, n_sn)),
                dma((12,)),
                dma((12,)),
                dma((4, 4)),
                dma((n_xl,)),
                dma((n_xl,)),
                dma((n_xl, n_xy)),
                dma((n_xl * n_xy,)),
                dma((zh, 2)),
                dma((n_z,)),
                dma((4, 2)),
                dma((4, 2)),
            ],
            compiler_params=pltpu.CompilerParams(
                collective_id=0, has_side_effects=True, vmem_limit_bytes=40 * 2**20
            ),
        )(*[pltpu.with_memory_space_constraint(v, pltpu.HBM) for v in (state, sketch, cell, row)])
        return pl.pallas_call(
            flush,
            out_shape=(
                jax.ShapeDtypeStruct(hank.shape, F32),
                jax.ShapeDtypeStruct(col.shape, F32),
            ),
            in_specs=[hbm] * 2,
            out_specs=(hbm, hbm),
            scratch_shapes=[dma((17,))],
            compiler_params=pltpu.CompilerParams(vmem_limit_bytes=2**20),
        )(hank, col)

    placed = (P("sensor", "tm"), P(), P("sensor", None, None), P("sensor", None, None))
    return jax.shard_map(
        local,
        mesh=mesh,
        in_specs=placed,
        out_specs=(P("tm", "sensor", None), P(("tm", "sensor"), None)),
        check_vma=False,
    )
```

```python
import functools
import math

import jax
import jax.numpy as jnp
from jax import lax
from jax.experimental import pallas as pl
from jax.experimental.pallas import tpu as pltpu
from jax.sharding import PartitionSpec as P

INPUTS = 16
KC = 64
LANES = 128
MESH = pl.DeviceIdType.MESH
AHEAD = 3
FIRST = 4 - AHEAD
F32 = jnp.float32
BF16 = jnp.bfloat16


def dot(a, b):
    return jnp.dot(a, b, preferred_element_type=F32)


def kernel(
    n_tm, n_sn, n_xl, n_xh, scale,
    state, sketch, cell, row, hank, col,
    st, sk, cellv, rowv, one, put, sendb, arr, hx, ht, big, hb, rb, acc2, tot, s0b, mid, s1b, m2, s2b,
    ld_sem, a_send, a_recv, h_send, h_recv, out_sem, s0_send, s0_recv, s1_send, s1_recv, s2_send, s2_recv,
):
    t = lax.axis_index("tm")
    s = lax.axis_index("sensor")
    n_z = n_tm // n_xl
    n_xy = n_sn // 2
    zh = n_z // 2
    xl = t // n_z
    z = lax.rem(t, n_z)
    xy = s // 2
    k = lax.rem(s, 2)
    cap = cellv.shape[2]
    sd = hx.shape[1]
    span = sk.shape[0]
    cells = st.shape[0]

    loads = [
        pltpu.make_async_copy(cell, cellv, ld_sem.at[0]),
        pltpu.make_async_copy(row, rowv, ld_sem.at[1]),
        pltpu.make_async_copy(state.at[:, pl.ds(0, 256)], st.at[:, pl.ds(0, 256)], ld_sem.at[2]),
        pltpu.make_async_copy(state.at[:, pl.ds(256, 256)], st.at[:, pl.ds(256, 256)], ld_sem.at[3]),
        pltpu.make_async_copy(sketch, sk, ld_sem.at[4]),
    ]
    for c in loads:
        c.start()

    barrier = pltpu.get_barrier_semaphore()

    def greet(tt, ss):
        pl.semaphore_signal(barrier, inc=1, device_id=(tt, ss), device_id_type=MESH)

    def greet_line(d, _):
        greet(xl * n_z + lax.rem(z + d, n_z), 2 * xy + z // zh)
        return 0

    def greet_sensor(d, _):
        greet(t, lax.rem(s + d, n_sn))
        return 0

    def greet_plane(b, _):
        greet(lax.rem(t + n_z, n_tm), 2 * b + k)
        return 0

    lax.fori_loop(1, n_sn, greet_sensor, 0)
    lax.fori_loop(1, n_z, greet_line, 0)
    lax.fori_loop(0, n_xy, greet_plane, 0)

    @pl.when(t < n_tm - 1)
    def _():
        greet(t + 1, s)

    @pl.when(t > 0)
    def _():
        greet(t - 1, s)

    n_greet = n_sn - 1 + n_xy + 2 * zh - jnp.where(z // zh == k, 2, 0)
    n_greet = n_greet + jnp.where(t > 0, 1, 0) + jnp.where(t < n_tm - 1, 1, 0)

    loads[0].wait()
    eye = lax.broadcasted_iota(jnp.int32, (cap, cap), 0) == lax.broadcasted_iota(jnp.int32, (cap, cap), 1)

    def column(ref, o):
        line = ref[0, o : o + 1, :].astype(F32)
        return jnp.sum(jnp.where(eye, jnp.broadcast_to(line, (cap, cap)), 0.0), axis=1, keepdims=True)

    lane_cells = lax.broadcasted_iota(jnp.int32, (cap, cells), 1).astype(F32)
    for o in range(n_sn):
        one[o * cap : (o + 1) * cap, :] = jnp.where(column(cellv, o) == lane_cells, 1.0, 0.0).astype(BF16)

    def pick(half):
        res = dot(one[...], st[:, 256 * half : 256 * half + 256]).astype(BF16)
        sendb[2 * half] = res[:, :LANES]
        sendb[2 * half + 1] = res[:, LANES:]

    def a_copy(q, d):
        dst = lax.rem(s + d, n_sn)
        return pltpu.make_async_remote_copy(
            src_ref=sendb.at[q, pl.ds(pl.multiple_of(dst * cap, cap), cap)],
            dst_ref=arr.at[q, pl.ds(pl.multiple_of(s * cap, cap), cap)],
            send_sem=a_send.at[q, d],
            recv_sem=a_recv.at[q, s],
            device_id=(t, dst),
            device_id_type=MESH,
        )

    def a_arrival(q, src):
        return pltpu.make_async_remote_copy(
            src_ref=sendb.at[q, pl.ds(pl.multiple_of(src * cap, cap), cap)],
            dst_ref=arr.at[q, pl.ds(pl.multiple_of(src * cap, cap), cap)],
            send_sem=a_send.at[q, 0],
            recv_sem=a_recv.at[q, src],
            device_id=(t, src),
            device_id_type=MESH,
        )

    def exchange(q):
        for d in sorted(range(1, n_sn), key=lambda d: (-min(d // 2 % 4, 4 - d // 2 % 4), d)):
            a_copy(q, d).start()
        own = pl.ds(pl.multiple_of(s * cap, cap), cap)
        arr[q, own] = sendb[q, own]

    loads[2].wait()
    pick(0)
    pl.semaphore_wait(barrier, n_greet)
    exchange(0)
    exchange(1)
    loads[3].wait()
    pick(1)
    exchange(2)
    exchange(3)

    loads[1].wait()
    lane_rows = lax.broadcasted_iota(jnp.int32, (cap, sd), 1).astype(F32)
    for o in range(n_sn):
        hit = jnp.where(column(rowv, o) == lane_rows, 1.0, 0.0).astype(BF16)
        one[o * cap : (o + 1) * cap, :sd] = hit
    put[...] = jnp.transpose(one[: n_sn * cap, :sd])

    loads[4].wait()
    for i in range(8):
        cols = pl.ds(LANES * i, LANES)
        if i > 0:
            big[: INPUTS * i, cols] = jnp.zeros((INPUTS * i, LANES), BF16)
        big[INPUTS * i : INPUTS * i + span, cols] = sk[...]
        big[INPUTS * i + span :, cols] = jnp.zeros((LANES - INPUTS * i, LANES), BF16)

    @pl.when(t >= n_tm - 2)
    def _():
        hx[12:16] = jnp.zeros((4, sd, LANES), BF16)
        ht[12 * LANES :, :] = jnp.zeros((4 * LANES, sd), BF16)

    @pl.when(t == n_tm - 1)
    def _():
        hx[8:12] = jnp.zeros((4, sd, LANES), BF16)
        ht[8 * LANES : 12 * LANES, :] = jnp.zeros((4 * LANES, sd), BF16)

    acc2[...] = jnp.zeros_like(acc2)

    def h_copy(src, dst, sem, to):
        return pltpu.make_async_remote_copy(
            src_ref=hx.at[src],
            dst_ref=hx.at[dst],
            send_sem=h_send.at[sem],
            recv_sem=h_recv.at[sem],
            device_id=(to, s),
            device_id_type=MESH,
        )

    before, after = jnp.maximum(t - 1, 0), jnp.minimum(t + 1, n_tm - 1)

    def down(q):
        return h_copy(4 + q, 8 + q, q, before)

    def onward(q):
        return h_copy(8 + q, 12 + q, 4 + q, before)

    def up(q):
        return h_copy(4 + q, q, 8 + q, after)

    def turn(c):
        ht[LANES * c : LANES * (c + 1), :] = jnp.transpose(hx[c])

    def place(q):
        def body(d, _):
            a_arrival(q, lax.rem(s + d, n_sn)).wait_recv()
            return 0

        lax.fori_loop(1, n_sn, body, 0)
        hx[4 + q] = dot(put[...], arr[q]).astype(BF16)

        @pl.when(t > 0)
        def _():
            down(q).start()

        if q >= FIRST:
            @pl.when(t < n_tm - 1)
            def _():
                up(q).start()

        turn(4 + q)

    def relay(q):
        @pl.when(t < n_tm - 1)
        def _():
            down(q).wait_recv()

            @pl.when(t > 0)
            def _():
                onward(q).start()

            turn(8 + q)

    def below(q):
        up(q).wait_recv()
        turn(q)

    def above(q):
        @pl.when(t < n_tm - 2)
        def _():
            onward(q).wait_recv()
            if 12 + q < 16 - AHEAD:
                turn(12 + q)

    def weigh(g, chunks, v):
        lhs = jnp.concatenate([hx[c] for c in chunks], axis=1)
        cols = slice(256 * v, 256 * v + 256)
        rhs = jnp.concatenate([big[LANES * (c - g) : LANES * (c - g + 1), cols] for c in chunks], axis=0)
        return dot(lhs, rhs)

    def part(g, chunks, first=False):
        for v in range(4):
            r = weigh(g, chunks, v)
            for i in range(2):
                piece = r[:, LANES * i : LANES * (i + 1)]
                hb[g, 2 * v + i] = piece if first else hb[g, 2 * v + i] + piece

    def last_part(g, chunks, rounded, kept):
        for v in range(4):
            r = weigh(g, chunks, v) + jnp.concatenate([hb[g, 2 * v], hb[g, 2 * v + 1]], axis=1)
            if kept:
                hb[g, 2 * v] = r[:, :LANES]
                hb[g, 2 * v + 1] = r[:, LANES:]
            if rounded:
                rb[v * sd : (v + 1) * sd, :] = r.astype(BF16)

    def out_copy(u, v):
        return pltpu.make_async_copy(
            hb.at[4 + u, pl.ds(2 * v, 2)], hank.at[pl.ds(8 * u + 2 * v, 2)], out_sem.at[u, v]
        )

    def image(g, low, high):
        lhs = jnp.concatenate(
            [ht[LANES * g + 32 * v + low : LANES * g + 32 * v + high, :] for v in range(4)], axis=1
        )
        acc2[low:high, :] = acc2[low:high, :] + dot(lhs, rb[...])

    full = span + INPUTS
    shared = list(range(4, 8 - AHEAD))
    ahead = list(range(FIRST, 4))
    later = list(range(8 - AHEAD, 8))

    place(0)
    place(1)
    for g in ahead + shared:
        part(g, [4, 5], True)
    place(2)
    place(3)
    relay(0)
    for g in ahead:
        part(g, [6, 7])
    relay(1)
    for g in shared:
        part(g, [6, 7])

    @pl.when(t == n_tm - 1)
    def _():
        for g in later:
            for v in range(4):
                rb[v * sd : (v + 1) * sd, :] = weigh(g, list(range(g, 8)), v).astype(BF16)
            image(g, 0, full)

    for g in ahead + shared:
        part(g, [8, 9])
    relay(2)

    @pl.when(t > 0)
    def _():
        below(1)
        below(2)
        part(1, [1, 2])
        part(2, [2, 10])
        below(3)
        last_part(1, [3], True, False)
        image(1, 0, full)

    relay(3)

    @pl.when(t > 0)
    def _():
        last_part(2, [3], True, False)
        image(2, 0, full)
        part(3, [10])
        last_part(3, [3, 11], True, False)
        image(3, 0, full)

    part(4, [10, 11])
    above(0)

    half_span = span // n_xl

    def s0_copy(a):
        return pltpu.make_async_remote_copy(
            src_ref=tot.at[a, pl.ds((1 - k) * zh, zh)],
            dst_ref=s0b.at[a],
            send_sem=s0_send.at[a],
            recv_sem=s0_recv.at[a],
            device_id=(t, s + 1 - 2 * k),
            device_id_type=MESH,
        )

    for g in shared:
        last_part(g, [12], True, True)
        for v in range(4):
            out_copy(g - 4, v).start()
        if g < shared[-1]:
            image(g, 0, full)
            continue
        for a in range(n_xl):
            low = half_span * a
            image(g, low + INPUTS if a else 0, low + half_span + INPUTS)
            whole = acc2[low : low + half_span, :LANES]
            whole = whole + acc2[low + INPUTS : low + half_span + INPUTS, LANES:]
            tot[a] = whole.reshape(tot.shape[1:])
            s0_copy(a).start()

    def part_later(rel, first):
        lhs = jnp.concatenate(
            [jnp.concatenate([hx[g + c] for c in rel], axis=1) for g in later], axis=0
        )
        for v in range(4):
            r = dot(lhs, big[LANES * rel[0] : LANES * (rel[-1] + 1), 256 * v : 256 * v + 256])
            for n, g in enumerate(later):
                for i in range(2):
                    piece = r[sd * n : sd * (n + 1), LANES * i : LANES * (i + 1)]
                    hb[g, 2 * v + i] = piece if first else hb[g, 2 * v + i] + piece
                if rel[-1] == 8:
                    out_copy(g - 4, v).start()

    part_later([0, 1], True)

    me = xl * n_xy + xy

    def s1_copy(a, b):
        return pltpu.make_async_remote_copy(
            src_ref=mid.at[a, b],
            dst_ref=s1b.at[me],
            send_sem=s1_send.at[a, b],
            recv_sem=s1_recv.at[me],
            device_id=(a * n_z + z, b * 2 + k),
            device_id_type=MESH,
        )

    def s1_arrival(e):
        return pltpu.make_async_remote_copy(
            src_ref=mid.at[0, 0],
            dst_ref=s1b.at[e],
            send_sem=s1_send.at[0, 0],
            recv_sem=s1_recv.at[e],
            device_id=(t, s),
            device_id_type=MESH,
        )

    for a in range(n_xl):
        s0_copy(a).wait_recv()
        for c in range(zh):
            mid[a, :, c] = tot[a, k * zh + c] + s0b[a, c]

        for d in sorted(range(n_xy), key=lambda d: -min(d % 4, 4 - d % 4)):
            b = lax.rem(xy + d, n_xy)
            if d:
                s1_copy(a, b).start()
            else:
                @pl.when(a != xl)
                def _():
                    s1_copy(a, b).start()


    s1b[me] = mid[xl, xy]
    part_later([2, 3, 4, 5], False)

    def s1_wait(d, _):
        s1_arrival(lax.rem(me + d, n_xl * n_xy)).wait_recv()
        return 0

    lax.fori_loop(1, n_xl * n_xy, s1_wait, 0)
    m2[...] = jnp.sum(s1b[...], axis=0)

    def s2_copy(c, kk):
        return pltpu.make_async_remote_copy(
            src_ref=m2.at[c],
            dst_ref=s2b.at[z],
            send_sem=s2_send.at[c, kk],
            recv_sem=s2_recv.at[z],
            device_id=(xl * n_z + k * zh + c, s - k + kk),
            device_id_type=MESH,
        )

    def s2_arrival(e):
        return pltpu.make_async_remote_copy(
            src_ref=m2.at[0],
            dst_ref=s2b.at[e],
            send_sem=s2_send.at[0, 0],
            recv_sem=s2_recv.at[e],
            device_id=(t, s),
            device_id_type=MESH,
        )

    for c in range(zh):
        for kk in range(2):
            @pl.when((k * zh + c != z) | (k != kk))
            def _():
                s2_copy(c, kk).start()

    @pl.when(z // zh == k)
    def _():
        s2b[z] = m2[z - k * zh]

    for g in later:
        above(g - 4)
    part_later([6, 7, 8], False)

    for q in range(4):
        def body(d, _):
            a_copy(q, d).wait_send()
            return 0

        lax.fori_loop(1, n_sn, body, 0)

    @pl.when(t > 0)
    def _():
        for q in range(4):
            down(q).wait_send()

    @pl.when(t < n_tm - 1)
    def _():
        for q in range(FIRST, 4):
            up(q).wait_send()

        @pl.when(t > 0)
        def _():
            for q in range(4):
                onward(q).wait_send()

    for a in range(n_xl):
        s0_copy(a).wait_send()

        def body(b, _):
            @pl.when((a != xl) | (b != xy))
            def _():
                s1_copy(a, b).wait_send()

            return 0

        lax.fori_loop(0, n_xy, body, 0)

    for e in range(n_z):
        @pl.when((e != z) | (z // zh != k))
        def _():
            s2_arrival(e).wait_recv()

    done = jnp.sum(s2b[...], axis=0)
    half = tot.shape[3] // 2
    col[...] = jnp.where(k == 0, done[:half], done[half:]) * scale

    for u in range(4):
        for v in range(4):
            out_copy(u, v).wait()
    for c in range(zh):
        for kk in range(2):
            @pl.when((k * zh + c != z) | (k != kk))
            def _():
                s2_copy(c, kk).wait_send()


def flush(hank, col, hank_out, col_out, sems):
    copies = [pltpu.make_async_copy(col, col_out, sems.at[0])]
    for u in range(16):
        part = pl.ds(2 * u, 2)
        copies.append(pltpu.make_async_copy(hank.at[part], hank_out.at[part], sems.at[1 + u]))
    for c in copies:
        c.start()
    for c in copies:
        c.wait()


def solution(mesh):
    n_tm, n_sn = mesh.shape["tm"], mesh.shape["sensor"]
    n_xl = 2
    n_z = n_tm // n_xl
    n_xy = n_sn // 2

    def local(state, sketch, cell, row):
        cells, width = state.shape
        span, cols = sketch.shape
        cap = cell.shape[2]
        sd = n_sn * cap // 2
        steps = width // INPUTS
        slots = n_sn * cap
        own_rows = span // (n_tm * n_sn)
        tr = 2 * own_rows
        zh = n_z // 2
        scale = 1.0 / math.sqrt(sd * n_sn * steps * n_tm)
        hbm = pl.BlockSpec(memory_space=pl.ANY)
        dma = pltpu.SemaphoreType.DMA
        hank, col = pl.pallas_call(
            functools.partial(kernel, n_tm, n_sn, n_xl, 1, scale),
            out_shape=(
                jax.ShapeDtypeStruct((steps, sd, cols), F32),
                jax.ShapeDtypeStruct((own_rows, cols), F32),
            ),
            in_specs=[hbm] * 4,
            out_specs=(hbm, pl.BlockSpec(memory_space=pltpu.VMEM)),
            scratch_shapes=[
                pltpu.VMEM((cells, width), BF16),
                pltpu.VMEM((span, cols), BF16),
                pltpu.VMEM(cell.shape, jnp.int32),
                pltpu.VMEM(row.shape, jnp.int32),
                pltpu.VMEM((slots, cells), BF16),
                pltpu.VMEM((sd, slots), BF16),
                pltpu.VMEM((4, slots, LANES), BF16),
                pltpu.VMEM((4, slots, LANES), BF16),
                pltpu.VMEM((16, sd, LANES), BF16),
                pltpu.VMEM((16 * LANES, sd), BF16),
                pltpu.VMEM((span + LANES, 8 * LANES), BF16),
                pltpu.VMEM((8, 8, sd, LANES), F32),
                pltpu.VMEM((4 * sd, 2 * LANES), BF16),
                pltpu.VMEM((span + INPUTS, 2 * LANES), F32),
                pltpu.VMEM((n_xl, n_z, n_xy, tr, LANES), F32),
                pltpu.VMEM((n_xl, zh, n_xy, tr, LANES), F32),
                pltpu.VMEM((n_xl, n_xy, zh, tr, LANES), F32),
                pltpu.VMEM((n_xl * n_xy, zh, tr, LANES), F32),
                pltpu.VMEM((zh, tr, LANES), F32),
                pltpu.VMEM((n_z, tr, LANES), F32),
                dma((5,)),
                dma((4, n_sn)),
                dma((4, n_sn)),
                dma((12,)),
                dma((12,)),
                dma((4, 4)),
                dma((n_xl,)),
                dma((n_xl,)),
                dma((n_xl, n_xy)),
                dma((n_xl * n_xy,)),
                dma((zh, 2)),
                dma((n_z,)),
            ],
            compiler_params=pltpu.CompilerParams(
                collective_id=0, has_side_effects=True, vmem_limit_bytes=40 * 2**20
            ),
        )(*[pltpu.with_memory_space_constraint(v, pltpu.HBM) for v in (state, sketch, cell, row)])
        return pl.pallas_call(
            flush,
            out_shape=(
                jax.ShapeDtypeStruct(hank.shape, F32),
                jax.ShapeDtypeStruct(col.shape, F32),
            ),
            in_specs=[hbm] * 2,
            out_specs=(hbm, hbm),
            scratch_shapes=[dma((17,))],
            compiler_params=pltpu.CompilerParams(vmem_limit_bytes=2**20),
        )(hank, col)

    placed = (P("sensor", "tm"), P(), P("sensor", None, None), P("sensor", None, None))
    return jax.shard_map(
        local,
        mesh=mesh,
        in_specs=placed,
        out_specs=(P("tm", "sensor", None), P(("tm", "sensor"), None)),
        check_vma=False,
    )
```
